32 devices in a mesh: groups: 2 (over y), seq: 4 (over z), head: 2 (over x), sub: 2 (over core).
Axes of the slice: x: 2, y: 2, z: 4, core: 2. Of those that a mesh axis runs over, the one named last changes fastest.
Arguments:
- tokens: int32 [3, 4096], P(None, ('groups', 'seq')), parts along dimension 1, may hold values from 0 to 1023
- masked: int32 [4096], P(('groups', 'seq')), parts along dimension 0, may hold values 0 or 1
- used_frames: int32 [2], P('groups'), parts along dimension 0, may hold values from 1024 to 2048
- tables: bfloat16 [3, 1024, 1024], P(None, None, ('head', 'sub')), may hold values from -6 to 6
- mask_vec: bfloat16 [1024], P(('head', 'sub')), may hold values from -6 to 6
- attn_in: bfloat16 [3, 1024, 512], P(None, None, ('head', 'sub')), may hold values from -0.1875 to 0.1875
- head_temp: float32 [8], P(('head', 'sub')), may hold values from 12 to 28
- attn_out: bfloat16 [512, 1024], P(('head', 'sub')), may hold values from -0.25 to 0.25
- conv_in: bfloat16 [2, 1024, 1024], P(None, None, ('head', 'sub')), may hold values from -0.1875 to 0.1875
- conv_kernel: float32 [31, 1024], P(None, ('head', 'sub')), may hold values from -1 to 1
- conv_out: bfloat16 [1024, 1024], P(('head', 'sub')), may hold values from -0.1875 to 0.1875
- voc_in: bfloat16 [1024, 512], P(('head', 'sub')), may hold values from -0.1875 to 0.1875
- voc_kernel: float32 [7, 512], replicated, may hold values from -2 to 2
- voc_up: bfloat16 [512, 1536], P(('head', 'sub')), may hold values from -0.25 to 0.25
- voc_down: bfloat16 [1536, 512], P(('head', 'sub')), may hold values from -0.15625 to 0.15625
- voc_head: bfloat16 [512, 1282], P(('head', 'sub')), may hold values from -0.25 to 0.25
- head_bias: float32 [1282], replicated, may hold values from 0.5 to 2.5
Outputs:
- features: bfloat16 [4096, 1024], P(('groups', 'seq', 'head', 'sub')), parts along dimension 0
- waveform: float32 [1310720], P(('groups', 'seq', 'head', 'sub')), parts along dimension 0
The draws below stay inside these ranges and needn't reach their ends.
There are 2 independent parts, one for each index of `groups`. The reference program is written for one: setup_inputs(seed, part) draws one part's arguments, and reference() takes and returns one part's arrays. A program takes and returns all parts, laid end to end along the dimension named above; an argument that names none is the same for every part. Nothing has to cross between parts.
All inputs are finite; a program needn't handle non-finite values. No bound on the sum of `masked` on one device may be relied on, other than what follows from the above.
Results may differ from the reference program's by a relative error of at most 0.02.
Values may be sent and summed in bfloat16 or wider, within the bound.
A program may use at most 64 MiB of HBM per device.

```python
import math
import jax
import jax.numpy as jnp
import numpy as np
from jax import lax

D = 1024
H = 8
CODES = 1024
KW = 31
VW = 512
VF = 1536
VK = 7
NFFT = 1280
HOP = 320
HW = 512
BINS = 641
L = 2048
N_SEQ = 4
N_HEAD = 2
N_SUB = 2


def set_ends(values, key, smallest, top_value):
    extent = values.shape
    spot = [jax.random.randint(jax.random.fold_in(key, axis), (), 0, extent[axis]) for axis in range(len(extent))]
    values = values.at[tuple(spot)].set(smallest)
    longest = extent.index(max(extent))
    spot[longest] = (spot[longest] + 1) % extent[longest]
    return values.at[tuple(spot)].set(top_value)


def levels(own_key, shape, shards, smallest, high):
    level = 1.0
    for axis_at, shards_of in shards:
        draws = jax.random.uniform(jax.random.fold_in(jax.random.fold_in(own_key, 6), axis_at), (shards_of,), jnp.float32, smallest / len(shards), high / len(shards))
        level = level * jnp.repeat(jnp.exp(draws), shape[axis_at] // shards_of).reshape((-1,) + (1,) * (len(shape) - 1 - axis_at))
    return level


def cumulative_ranks(amount, lean):
    loads = [(1 << 20) // math.isqrt(rank ** lean) + 1 for rank in range(1, amount + 1)]
    spread = 1 + sum(loads) // (1 << 30)
    return np.cumsum(np.array([max(1, weight // spread) for weight in loads]))


def ranked(rng, dims, number_of, skew):
    table = cumulative_ranks(number_of, skew)
    lot = jax.random.randint(jax.random.fold_in(rng, 1), dims, 0, int(table[number_of - 1]))
    rank = jnp.searchsorted(jnp.asarray(table, jnp.int32), lot, side="right")
    return jax.random.permutation(jax.random.fold_in(rng, 2), number_of)[rank].astype(jnp.int32)


def centred(own_key, shape, scale, most, split=(), kind=jnp.bfloat16):
    array = jax.random.normal(own_key, shape, jnp.float32) * scale
    if len(split) > 0:
        array = levels(own_key, shape, split, -0.22, 0.18) * array
    return jnp.clip(array, min=-most, max=most).astype(kind)


def setup_inputs(seed: int = 0, part: int = 0) -> dict:
    keys = jax.random.split(jax.random.key(seed), 18)
    part_splits = jax.random.split(jax.random.fold_in(keys[17], part), 18)
    return {
        "tokens": set_ends(ranked(part_splits[0], (3, L), CODES, 2), jax.random.fold_in(part_splits[0], 3), 0, CODES - 1).astype(jnp.int32),
        "masked": set_ends((jax.random.randint(part_splits[1], (L,), 0, 2) < 1).astype(jnp.int32), jax.random.fold_in(part_splits[1], 1), 0, 1),
        "used_frames": jax.random.randint(part_splits[2], (1,), L // 2, L + 1).astype(jnp.int32),
        "tables": centred(keys[3], (3, CODES, D), 1.0, 6.0, ((2, 4),)),
        "mask_vec": centred(keys[4], (D,), 1.0, 6.0, ((0, 4),)),
        "attn_in": centred(keys[5], (3, D, HW), D ** -0.5, 0.1875, ((2, 4),)),
        "head_temp": jnp.clip(jnp.exp(math.log(28.0) - 0.84729786 * jax.random.uniform(keys[6], (H,), jnp.float32) ** levels(keys[6], (H,), ((0, 4),), -0.2, 0.2)), 12.0, 28.0),
        "attn_out": centred(keys[7], (HW, D), HW ** -0.5, 0.25, ((0, 4),)),
        "conv_in": centred(keys[8], (2, D, D), D ** -0.5, 0.1875, ((2, 4),)),
        "conv_kernel": centred(keys[9], (KW, D), KW ** -0.5, 1.0, ((1, 4),), jnp.float32),
        "conv_out": centred(keys[10], (D, D), D ** -0.5, 0.1875, ((0, 4),)),
        "voc_in": centred(keys[11], (D, VW), D ** -0.5, 0.1875, ((0, 4),)),
        "voc_kernel": centred(keys[12], (VK, VW), VK ** -0.5, 2.0, (), jnp.float32),
        "voc_up": centred(keys[13], (VW, VF), VW ** -0.5, 0.25, ((0, 4),)),
        "voc_down": centred(keys[14], (VF, VW), VF ** -0.5, 0.15625, ((0, 4),)),
        "voc_head": centred(keys[15], (VW, 2 * BINS), VW ** -0.5, 0.25, ((0, 4),)),
        "head_bias": jnp.clip(jax.random.uniform(keys[16], (2 * BINS,), jnp.float32, 0.5, 2.5), 0.5, 2.5),
    }


def layer_norm(values):
    average = lax.optimization_barrier(jnp.mean(values, axis=-1, keepdims=True))
    centered = values - average
    return centered * lax.rsqrt(lax.optimization_barrier(jnp.mean(centered * centered, axis=-1, keepdims=True)) + 1e-05)

def unit_heads(projected, head_count):
    row_count = projected.shape[0]
    split_heads = projected.reshape(row_count, head_count, projected.shape[1] // head_count)
    scaled = split_heads * lax.rsqrt(lax.optimization_barrier(jnp.sum(split_heads * split_heads, axis=-1, keepdims=True)) + 1e-06)
    return scaled.astype(jnp.bfloat16)

def depthwise(kernel, rows_in):
    tap_count = kernel.shape[0]
    half_taps = tap_count // 2
    padded_rows = jnp.pad(rows_in.astype(jnp.float32), ((half_taps, half_taps), (0, 0)))
    out_rows = rows_in.shape[0]
    result = jnp.zeros((out_rows, rows_in.shape[1]), jnp.float32)
    for offset in range(tap_count):
        result = result + kernel[offset].astype(jnp.float32) * padded_rows[offset:offset + out_rows]
    return result

def reference(tokens, masked, used_frames, tables, mask_vec, attn_in, head_temp, attn_out, conv_in, conv_kernel, conv_out, voc_in, voc_kernel, voc_up, voc_down, voc_head, head_bias):
    total_frames = tokens.shape[1]
    masked_rows = masked == 1
    level_two = jnp.where(masked_rows[:, None], mask_vec.astype(jnp.float32)[None, :], tables[2][tokens[2]].astype(jnp.float32))
    embedded = (tables[0][tokens[0]].astype(jnp.float32) + tables[1][tokens[1]].astype(jnp.float32) + level_two).astype(jnp.bfloat16)
    normed = layer_norm(embedded.astype(jnp.float32)).astype(jnp.bfloat16)
    head_count = head_temp.shape[0]
    query_normalized = unit_heads(jnp.dot(normed, attn_in[0], preferred_element_type=jnp.float32), head_count)
    key_unit = unit_heads(jnp.dot(normed, attn_in[1], preferred_element_type=jnp.float32), head_count)
    value_rows = jnp.dot(normed, attn_in[2], preferred_element_type=jnp.float32).astype(jnp.bfloat16)
    value_heads = value_rows.reshape(total_frames, head_count, -1)
    lookup_admissible_flags = jnp.arange(total_frames) < used_frames[0]
    block_rows = total_frames // N_SEQ

    def one_head(attender_element):
        asker_vectors_split, lookup_vectors_split, content_vectors_split, similarity_sharpness = attender_element

        def one_block(query_block):
            angular_similarity = jnp.dot(query_block, lookup_vectors_split.T, preferred_element_type=jnp.float32)
            attention_probabilities = jnp.where(lookup_admissible_flags[None, :], jnp.exp(similarity_sharpness * (angular_similarity - 1.0)), 0.0)
            normalizer = lax.optimization_barrier(jnp.sum(attention_probabilities, axis=1, keepdims=True))
            weighted = jnp.dot(attention_probabilities.astype(jnp.bfloat16), content_vectors_split, preferred_element_type=jnp.float32)
            return weighted / normalizer
        blocks_out = lax.map(one_block, asker_vectors_split.reshape(N_SEQ, block_rows, asker_vectors_split.shape[1]))
        return blocks_out.reshape(total_frames, asker_vectors_split.shape[1])
    per_head = lax.map(one_head, (jnp.transpose(query_normalized, (1, 0, 2)), jnp.transpose(key_unit, (1, 0, 2)), jnp.transpose(value_heads, (1, 0, 2)), head_temp))
    attended = jnp.transpose(per_head, (1, 0, 2)).reshape(total_frames, -1).astype(jnp.bfloat16)
    stream = embedded.astype(jnp.float32) + jnp.dot(attended, attn_out, preferred_element_type=jnp.float32)
    conv_normed = layer_norm(stream).astype(jnp.bfloat16)
    gate_value = jnp.dot(conv_normed, conv_in[0], preferred_element_type=jnp.float32)
    gate_signal = jnp.dot(conv_normed, conv_in[1], preferred_element_type=jnp.float32)
    gated_rows = (gate_value * jax.nn.sigmoid(gate_signal)).astype(jnp.bfloat16)
    depth_rows = depthwise(conv_kernel, gated_rows)
    activated = (depth_rows * jax.nn.sigmoid(depth_rows)).astype(jnp.bfloat16)
    group_count = N_HEAD * N_SUB
    channels = activated.shape[1] // group_count
    conv_sum = jnp.zeros(stream.shape, jnp.float32)
    for member in range(group_count):
        group_part = jnp.dot(activated[:, member * channels:(member + 1) * channels], conv_out[member * channels:(member + 1) * channels], preferred_element_type=jnp.float32).astype(jnp.bfloat16)
        conv_sum = conv_sum + lax.optimization_barrier(group_part).astype(jnp.float32)
    features = layer_norm(stream + conv_sum).astype(jnp.bfloat16)
    live_rows = (jnp.arange(total_frames) < used_frames[0])[:, None]
    base_rows = layer_norm(jnp.where(live_rows, jnp.dot(features, voc_in, preferred_element_type=jnp.float32), 0.0))
    vdepth = depthwise(voc_kernel, base_rows)
    inner_rows = layer_norm(vdepth).astype(jnp.bfloat16)
    hidden = jax.nn.gelu(jnp.dot(inner_rows, voc_up, preferred_element_type=jnp.float32), approximate=False).astype(jnp.bfloat16)
    refined = base_rows + jnp.dot(hidden, voc_down, preferred_element_type=jnp.float32)
    head_input = layer_norm(refined).astype(jnp.bfloat16)
    spectrum = jnp.dot(head_input, voc_head, preferred_element_type=jnp.float32) + head_bias
    bin_count = spectrum.shape[1] // 2
    magnitude = jnp.minimum(jnp.exp(spectrum[:, :bin_count]), 100.0)
    phase_rows = spectrum[:, bin_count:]
    real_part = magnitude * jnp.cos(phase_rows)
    imag_part = magnitude * jnp.sin(phase_rows)
    wave_rows = jnp.fft.irfft(lax.complex(real_part, imag_part), n=NFFT, axis=1)
    sample_ids = jnp.arange(NFFT).astype(jnp.float32)
    hann_window = 0.5 - 0.5 * jnp.cos(2.0 * math.pi / NFFT * sample_ids)
    intersection = NFFT // HOP
    framed = (wave_rows * hann_window[None, :]).reshape(total_frames, intersection, HOP)
    envelope = jnp.broadcast_to((hann_window * hann_window).reshape(1, intersection, HOP), framed.shape)
    padded_frames = jnp.pad(framed, ((intersection, intersection), (0, 0), (0, 0)))
    padded_env = jnp.pad(envelope, ((intersection, intersection), (0, 0), (0, 0)))
    audio_sum = jnp.zeros((total_frames, HOP), jnp.float32)
    energy = jnp.zeros((total_frames, HOP), jnp.float32)
    for quarter in range(intersection):
        begin = intersection + intersection // 2 - quarter
        audio_sum = audio_sum + padded_frames[begin:begin + total_frames, quarter]
        energy = energy + padded_env[begin:begin + total_frames, quarter]
    waveform = (audio_sum / energy).reshape(total_frames * HOP)
    return (features, waveform)
```

```python
import functools
import math

import jax
import jax.numpy as jnp
from jax import lax
from jax.experimental import pallas as pl
from jax.experimental.pallas import tpu as pltpu
from jax.sharding import PartitionSpec as P

HOP = 320


def layer_norm(values):
    average = jnp.mean(values, axis=-1, keepdims=True)
    centered = values - average
    return centered * lax.rsqrt(jnp.mean(centered * centered, axis=-1, keepdims=True) + 1e-05)


def depthwise(kernel, padded_rows):
    tap_count = kernel.shape[0]
    out_rows = padded_rows.shape[0] - tap_count + 1
    result = jnp.zeros((out_rows, padded_rows.shape[1]), jnp.float32)
    for offset in range(tap_count):
        result = result + kernel[offset] * padded_rows[offset : offset + out_rows].astype(
            jnp.float32
        )
    return result


def synthesis_tables(bin_count, fft_size, window):
    fine = 16
    coarse = -(-bin_count // fine)
    unit = 2.0 * math.pi / fft_size
    samples = lax.broadcasted_iota(jnp.int32, (coarse, fft_size), 1)
    steps = lax.broadcasted_iota(jnp.int32, (coarse, fft_size), 0) * fine
    big = unit * (steps * samples % fft_size).astype(jnp.float32)
    samples = lax.broadcasted_iota(jnp.int32, (fine, fft_size), 1)
    steps = lax.broadcasted_iota(jnp.int32, (fine, fft_size), 0)
    small = unit * (steps * samples % fft_size).astype(jnp.float32)
    big_cos, big_sin, small_cos, small_sin = lax.optimization_barrier(
        (jnp.cos(big) * window, jnp.sin(big) * window, jnp.cos(small), jnp.sin(small))
    )
    cosine = big_cos[:, None] * small_cos[None] - big_sin[:, None] * small_sin[None]
    sine = big_sin[:, None] * small_cos[None] + big_cos[:, None] * small_sin[None]
    bins = lax.broadcasted_iota(jnp.int32, (coarse * fine, 1), 0)
    edge = (bins == 0) | (bins == bin_count - 1)
    factor = jnp.where(edge, 1.0, 2.0) / fft_size
    cosine = factor * cosine.reshape(coarse * fine, fft_size)
    sine = jnp.where(edge, 0.0, -factor * sine.reshape(coarse * fine, fft_size))
    return cosine[:bin_count].astype(jnp.bfloat16), sine[:bin_count].astype(jnp.bfloat16)


MESH = pl.DeviceIdType.MESH
HALO = 32


def remote(src, dst, send_sem, recv_sem, **where):
    return pltpu.make_async_remote_copy(
        src_ref=src,
        dst_ref=dst,
        send_sem=send_sem,
        recv_sem=recv_sem,
        device_id=where,
        device_id_type=MESH,
    )


class Place:
    def __init__(self):
        self.group, self.seq = lax.axis_index("groups"), lax.axis_index("seq")
        self.head, self.sub = lax.axis_index("head"), lax.axis_index("sub")
        self.groups, self.seqs = lax.axis_size("groups"), lax.axis_size("seq")
        self.heads = lax.axis_size("head")
        self.me = self.head * 2 + self.sub
        self.partner = 1 - self.sub

    def head_at(self, step):
        return lax.rem(self.head + step, self.heads)

    def group_at(self, step):
        return lax.rem(self.group + step, self.groups)


def enter(at, with_seq):
    barrier = pltpu.get_barrier_semaphore()
    for step in range(1, at.heads):
        pl.semaphore_signal(barrier, inc=1, device_id={"head": at.head_at(step)}, device_id_type=MESH)
    for step in range(1, at.groups):
        pl.semaphore_signal(barrier, inc=1, device_id={"groups": at.group_at(step)}, device_id_type=MESH)
    pl.semaphore_signal(barrier, inc=1, device_id={"sub": at.partner}, device_id_type=MESH)
    count = at.heads + at.groups - 1
    if with_seq:

        @pl.when(at.seq > 0)
        def _():
            pl.semaphore_signal(barrier, inc=1, device_id={"seq": at.seq - 1}, device_id_type=MESH)

        @pl.when(at.seq < at.seqs - 1)
        def _():
            pl.semaphore_signal(barrier, inc=1, device_id={"seq": at.seq + 1}, device_id_type=MESH)

        count = (
            count
            + jnp.where(at.seq > 0, 1, 0)
            + jnp.where(at.seq < at.seqs - 1, 1, 0)
        )
    pl.semaphore_wait(barrier, count)


class Spread:
    def __init__(self, at, buffer, rows, sems):
        self.at, self.buffer, self.rows = at, buffer, rows
        self.send, self.recv = sems

    def part(self, block):
        return self.buffer.at[block, pl.ds(*self.rows)]

    def cross(self, step):
        block = self.part(self.at.me)
        return remote(
            block, block, self.send.at[step], self.recv.at[step], head=self.at.head_at(step)
        )

    def aside(self, step):
        block = self.part(self.at.head_at(self.at.heads - step) * 2 + self.at.sub)
        slot = self.at.heads + step
        return remote(block, block, self.send.at[slot], self.recv.at[slot], sub=self.at.partner)

    def start(self):
        for step in range(1, self.at.heads):
            self.cross(step).start()
        self.aside(0).start()

    def relay(self):
        for step in range(1, self.at.heads):
            self.cross(step).wait_recv()
            self.aside(step).start()

    def finish(self):
        for step in range(self.at.heads):
            if step > 0:
                self.cross(step).wait_send()
            self.aside(step).wait()


class Weight:
    def __init__(self, at, own, full, sems):
        self.at, self.own, self.full = at, own, full
        self.send, self.recv, self.local = sems
        self.length = own.shape[0] // at.groups

    def piece(self, block, part):
        start = pl.multiple_of(part * self.length, 16)
        return self.full.at[block, pl.ds(start, self.length)]

    def source(self, step):
        return self.at.head_at(self.at.heads - step) * 2 + self.at.sub

    def cross(self, step):
        start = pl.multiple_of(self.at.group * self.length, 16)
        return remote(
            self.own.at[pl.ds(start, self.length)],
            self.piece(self.at.me, self.at.group),
            self.send.at[step],
            self.recv.at[step],
            head=self.at.head_at(step),
        )

    def over(self, step, turn):
        block = self.piece(self.source(step), self.at.group)
        slot = self.at.heads + (step - 1) * self.at.groups + turn
        return remote(
            block, block, self.send.at[slot], self.recv.at[slot], groups=self.at.group_at(turn)
        )

    def aside(self, step, turn):
        part = self.at.group_at(self.at.groups - turn)
        block = self.piece(self.source(step), part)
        slot = self.at.heads * (1 + self.at.groups) + (step - 1) * self.at.groups + turn
        return remote(block, block, self.send.at[slot], self.recv.at[slot], sub=self.at.partner)

    def mine(self):
        return remote(
            self.own, self.full.at[self.at.me], self.send.at[0], self.recv.at[0], sub=self.at.partner
        )

    def kept(self):
        return pltpu.make_async_copy(self.own, self.full.at[self.at.me], self.local.at[0])

    def start(self):
        for step in range(1, self.at.heads):
            self.cross(step).start()
        self.mine().start()
        self.kept().start()

    def relay_cross(self):
        for step in range(1, self.at.heads):
            self.cross(step).wait_recv()
            for turn in range(1, self.at.groups):
                self.over(step, turn).start()
            self.aside(step, 0).start()

    def relay_over(self):
        for step in range(1, self.at.heads):
            for turn in range(1, self.at.groups):
                self.over(step, turn).wait_recv()
                self.aside(step, turn).start()

    def finish(self):
        self.mine().wait()
        self.kept().wait()
        for step in range(1, self.at.heads):
            self.cross(step).wait_send()
            for turn in range(1, self.at.groups):
                self.over(step, turn).wait_send()
            for turn in range(self.at.groups):
                self.aside(step, turn).wait()


def weight_sems(heads, groups):
    count = heads * (1 + 2 * groups)
    return [
        pltpu.SemaphoreType.DMA((count,)),
        pltpu.SemaphoreType.DMA((count,)),
        pltpu.SemaphoreType.DMA((1,)),
    ]


def norm_rows(values):
    average = jnp.mean(values, axis=-1, keepdims=True)
    centered = values - average
    return centered * lax.rsqrt(jnp.mean(centered * centered, axis=-1, keepdims=True) + 1e-05)


def attention_kernel(weight_count, head_size, *refs):
    used_ref, temp_ref, tok_ref, tables_ref, mask_ref, attn_ref = refs[:6]
    owns = refs[6 : 6 + weight_count]
    refs = refs[6 + weight_count :]
    emb_out, att_out = refs[:2]
    fulls = refs[2 : 2 + weight_count]
    refs = refs[2 + weight_count :]
    (tokh, emb, att, kvbuf, q_scr, acc, l_acc, tok_send, tok_recv, e_send, e_recv, a_send, a_recv,
     r_send, r_recv, l_send, l_recv) = refs[:17]
    wsems = refs[17:]
    at = Place()
    rows = tok_ref.shape[0]
    total = rows + 2 * HALO
    blocks = emb.shape[0]
    codes = tables_ref.shape[1]
    local_heads = q_scr.shape[0]
    width = q_scr.shape[2]
    tokh[...] = jnp.zeros_like(tokh)
    enter(at, True)
    first, last = at.seq == 0, at.seq == at.seqs - 1

    def tokens_up():
        return remote(tok_ref.at[pl.ds(rows - HALO, HALO)], tokh.at[pl.ds(0, HALO)],
                      tok_send.at[0], tok_recv.at[0], seq=at.seq + 1)

    def tokens_down():
        return remote(tok_ref.at[pl.ds(0, HALO)], tokh.at[pl.ds(HALO, HALO)],
                      tok_send.at[1], tok_recv.at[1], seq=at.seq - 1)

    @pl.when(jnp.logical_not(last))
    def _():
        tokens_up().start()

    @pl.when(jnp.logical_not(first))
    def _():
        tokens_down().start()

    weights = [
        Weight(at, owns[w], fulls[w], wsems[3 * w : 3 * w + 3]) for w in range(weight_count)
    ]

    def embed(token_rows):
        count = token_rows.shape[0]
        ids = lax.broadcasted_iota(jnp.int32, (count, codes), 1)
        result = token_rows[:, 3:4].astype(jnp.float32) * mask_ref[...].astype(jnp.float32)
        for level in range(3):
            hot = jnp.where(token_rows[:, level : level + 1] == ids, 1.0, 0.0).astype(jnp.bfloat16)
            result = result + jnp.dot(hot, tables_ref[level], preferred_element_type=jnp.float32)
        return result.astype(jnp.bfloat16)

    half = rows // 2
    cut = half // 2
    spreads = [
        Spread(at, emb, (0, half), (e_send.at[0], e_recv.at[0])),
        Spread(at, emb, (half, total - half), (e_send.at[1], e_recv.at[1])),
    ]
    for chunk in range(2):
        emb[at.me, pl.ds(chunk * cut, cut)] = embed(tok_ref[pl.ds(chunk * cut, cut)])
    spreads[0].start()
    for chunk in range(2, 4):
        emb[at.me, pl.ds(chunk * cut, cut)] = embed(tok_ref[pl.ds(chunk * cut, cut)])

    @pl.when(jnp.logical_not(last))
    def _():
        tokens_up().wait_send()

    @pl.when(jnp.logical_not(first))
    def _():
        tokens_up().wait_recv()
        tokens_down().wait_send()

    @pl.when(jnp.logical_not(last))
    def _():
        tokens_down().wait_recv()

    emb[at.me, pl.ds(rows, 2 * HALO)] = embed(tokh[...])
    spreads[1].start()
    for weight in weights:
        weight.start()

    lanes = lax.broadcasted_iota(jnp.int32, (1, width), 1)
    in_head = [
        (lanes >= h * head_size) & (lanes < (h + 1) * head_size) for h in range(local_heads)
    ]

    def unit(projected):
        squares = projected * projected
        scale = jnp.zeros_like(projected)
        for h in range(local_heads):
            total_h = jnp.sum(jnp.where(in_head[h], squares, 0.0), axis=-1, keepdims=True)
            scale = jnp.where(in_head[h], lax.rsqrt(total_h + 1e-06), scale)
        return projected * scale

    own_kv = kvbuf.at[at.seq]
    step_rows = 64
    for index, spread in enumerate(spreads):
        spread.relay()
        spread.finish()
        begin, count = spread.rows
        piece = count // 2 if count // 2 % 32 == 0 else count
        for offset in range(begin, begin + count, piece):
            size = piece
            whole = jnp.concatenate(
                [emb[block, pl.ds(offset, size)] for block in range(blocks)], axis=1
            )
            emb_out[pl.ds(offset, size)] = whole
            normed = norm_rows(whole.astype(jnp.float32)).astype(jnp.bfloat16)
            query = unit(jnp.dot(normed, attn_ref[0], preferred_element_type=jnp.float32))
            for h in range(local_heads):
                q_scr[h, pl.ds(offset, size)] = jnp.where(in_head[h], query, 0.0).astype(jnp.bfloat16)
            kept = min(size, rows - offset)
            if kept > 0:
                normed = normed[:kept]
                own_kv[0, pl.ds(offset, kept)] = unit(
                    jnp.dot(normed, attn_ref[1], preferred_element_type=jnp.float32)
                ).astype(jnp.bfloat16)
                own_kv[1, pl.ds(offset, kept)] = jnp.dot(
                    normed, attn_ref[2], preferred_element_type=jnp.float32
                ).astype(jnp.bfloat16)

    def send_up(block, step):
        view = kvbuf.at[block]
        return remote(view, view, r_send.at[step], r_recv.at[step], seq=at.seq + 1)

    def send_down(block, step):
        view = kvbuf.at[block]
        return remote(view, view, l_send.at[step], l_recv.at[step], seq=at.seq - 1)

    @pl.when(jnp.logical_not(last))
    def _():
        send_up(at.seq, 0).start()

    @pl.when(jnp.logical_not(first))
    def _():
        send_down(at.seq, 0).start()

    acc[...] = jnp.zeros_like(acc)
    l_acc[...] = jnp.zeros_like(l_acc)
    tile = total // 3

    def attend(block):
        frame = block * rows + lax.broadcasted_iota(jnp.int32, (1, rows), 1)
        live = frame < used_ref[0]
        for h in range(local_heads):
            sharp = temp_ref[h] * 1.4426950408889634
            bias = jnp.where(live, -sharp, -1e30)

            def one(index, carry):
                span = pl.ds(pl.multiple_of(index * tile, 64), tile)
                scores = lax.dot_general(
                    q_scr[h, span],
                    kvbuf[block, 0],
                    (((1,), (1,)), ((), ())),
                    preferred_element_type=jnp.float32,
                )
                chance = jnp.exp2(scores * sharp + bias)
                part = chance[:, :128]
                for lane in range(128, rows, 128):
                    part = part + chance[:, lane : lane + 128]
                l_acc[h, span] += part
                acc[h, span] += jnp.dot(
                    chance.astype(jnp.bfloat16), kvbuf[block, 1], preferred_element_type=jnp.float32
                )
                return carry

            lax.fori_loop(0, 3, one, 0)

    def exchange(step):
        @pl.when(step < at.seq)
        def _():
            block = at.seq - 1 - step
            send_up(block, step).wait_recv()

            @pl.when(jnp.logical_not(last))
            def _():
                send_up(block, step + 1).start()

            attend(block)

        @pl.when(step < at.seqs - 1 - at.seq)
        def _():
            block = at.seq + 1 + step
            send_down(block, step).wait_recv()

            @pl.when(jnp.logical_not(first))
            def _():
                send_down(block, step + 1).start()

            attend(block)

    attend(at.seq)
    weights[0].relay_cross()
    if at.seqs > 1:
        exchange(0)
    weights[0].relay_over()
    for weight in weights[1:2]:
        weight.relay_cross()

    def later(step, carry):
        exchange(step)
        return carry

    lax.fori_loop(1, at.seqs - 1, later, 0)
    value = jnp.zeros((total, width), jnp.float32)
    for h in range(local_heads):
        mean = acc[h] / jnp.sum(l_acc[h], axis=-1, keepdims=True)
        value = jnp.where(in_head[h], mean, value)
    att[at.me] = value.astype(jnp.bfloat16)
    gather = Spread(at, att, (0, total), (a_send, a_recv))
    gather.start()
    for weight in weights[2:]:
        weight.relay_cross()
    for weight in weights[1:]:
        weight.relay_over()
    gather.relay()

    def drain(step, carry):
        @pl.when(jnp.logical_not(last) & (step <= at.seq))
        def _():
            send_up(at.seq - step, step).wait_send()

        @pl.when(jnp.logical_not(first) & (step <= at.seqs - 1 - at.seq))
        def _():
            send_down(at.seq + step, step).wait_send()

        return carry

    lax.fori_loop(0, at.seqs - 1, drain, 0)
    gather.finish()
    for block in range(blocks):
        att_out[block] = att[block]
    for weight in weights:
        weight.finish()


def attention(used_frames, head_temp, packed, tables, mask_vec, attn_in, owns, blocks):
    groups, heads, seqs = (lax.axis_size(name) for name in ("groups", "head", "seq"))
    rows = packed.shape[0]
    total = rows + 2 * HALO
    width = attn_in.shape[2]
    local_heads = head_temp.shape[0]
    columns = tables.shape[2]
    vmem = pl.BlockSpec(memory_space=pltpu.VMEM)
    smem = pl.BlockSpec(memory_space=pltpu.SMEM)
    dma = pltpu.SemaphoreType.DMA
    sems = []
    for _ in owns:
        sems += weight_sems(heads, groups)
    return pl.pallas_call(
        functools.partial(attention_kernel, len(owns), width // local_heads),
        out_shape=[
            jax.ShapeDtypeStruct((total, columns * blocks), jnp.bfloat16),
            jax.ShapeDtypeStruct((blocks, total, width), jnp.bfloat16),
        ]
        + [jax.ShapeDtypeStruct((blocks,) + own.shape, own.dtype) for own in owns],
        in_specs=[smem, smem] + [vmem] * (4 + len(owns)),
        out_specs=[vmem, vmem] + [pl.BlockSpec(memory_space=pl.ANY)] * len(owns),
        scratch_shapes=[
            pltpu.VMEM((2 * HALO, packed.shape[1]), jnp.int32),
            pltpu.VMEM((blocks, total, columns), jnp.bfloat16),
            pltpu.VMEM((blocks, total, width), jnp.bfloat16),
            pltpu.VMEM((seqs, 2, rows, width), jnp.bfloat16),
            pltpu.VMEM((local_heads, total, width), jnp.bfloat16),
            pltpu.VMEM((local_heads, total, width), jnp.float32),
            pltpu.VMEM((local_heads, total, 128), jnp.float32),
            dma((2,)),
            dma((2,)),
            dma((2, 2 * heads)),
            dma((2, 2 * heads)),
            dma((2 * heads,)),
            dma((2 * heads,)),
            dma((seqs,)),
            dma((seqs,)),
            dma((seqs,)),
            dma((seqs,)),
        ]
        + sems,
        compiler_params=pltpu.CompilerParams(collective_id=0, has_side_effects=True, vmem_limit_bytes=60 * 1024 * 1024),
    )(used_frames, head_temp, packed, tables, mask_vec.reshape(1, -1), attn_in, *owns)


def swap_kernel(weight_count, *refs):
    win_ref = refs[0]
    owns = refs[1 : 1 + weight_count]
    out_ref = refs[1 + weight_count]
    fulls = refs[2 + weight_count : 2 + 2 * weight_count]
    act, send, recv = refs[2 + 2 * weight_count : 5 + 2 * weight_count]
    wsems = refs[5 + 2 * weight_count :]
    at = Place()
    blocks = at.heads * 2
    barrier = pltpu.get_barrier_semaphore()
    peers = []
    for step in range(at.heads):
        for other in range(2):
            if step or other:
                peers.append((step, other))
    for step, other in peers:
        pl.semaphore_signal(
            barrier,
            inc=1,
            device_id={"head": at.head_at(step), "sub": lax.rem(at.sub + other, 2)},
            device_id_type=MESH,
        )
    for step in range(1, at.groups):
        pl.semaphore_signal(barrier, inc=1, device_id={"groups": at.group_at(step)}, device_id_type=MESH)
    pl.semaphore_wait(barrier, blocks - 1 + at.groups - 1)
    copies = []
    for slot, (step, other) in enumerate(peers):
        head, sub = at.head_at(step), lax.rem(at.sub + other, 2)
        copies.append(
            remote(win_ref.at[head * 2 + sub], act.at[at.me], send.at[slot], recv.at[slot], head=head, sub=sub)
        )
        copies[-1].start()
    weights = [
        Weight(at, owns[w], fulls[w], wsems[3 * w : 3 * w + 3]) for w in range(weight_count)
    ]
    for weight in weights:
        weight.start()
    act[at.me] = win_ref[at.me]
    for weight in weights:
        weight.relay_cross()
    for weight in weights:
        weight.relay_over()
    for slot, (step, other) in enumerate(peers):
        copies[slot].wait_send()
        source = at.head_at(at.heads - step) * 2 + lax.rem(at.sub + other, 2)
        remote(win_ref.at[source], act.at[source], send.at[slot], recv.at[slot],
               head=at.head_at(step), sub=lax.rem(at.sub + other, 2)).wait_recv()
    out_ref[...] = act[...]
    for weight in weights:
        weight.finish()


def swap(windows, owns):
    groups, heads = lax.axis_size("groups"), lax.axis_size("head")
    vmem = pl.BlockSpec(memory_space=pltpu.VMEM)
    dma = pltpu.SemaphoreType.DMA
    sems = []
    for _ in owns:
        sems += weight_sems(heads, groups)
    blocks = windows.shape[0]
    return pl.pallas_call(
        functools.partial(swap_kernel, len(owns)),
        out_shape=[jax.ShapeDtypeStruct(windows.shape, windows.dtype)]
        + [jax.ShapeDtypeStruct((blocks,) + own.shape, own.dtype) for own in owns],
        in_specs=[vmem] * (1 + len(owns)),
        out_specs=[vmem] + [pl.BlockSpec(memory_space=pl.ANY)] * len(owns),
        scratch_shapes=[
            pltpu.VMEM(windows.shape, windows.dtype),
            dma((blocks,)),
            dma((blocks,)),
        ]
        + sems,
        compiler_params=pltpu.CompilerParams(collective_id=1, has_side_effects=True),
    )(windows, *owns)


def local(
    tokens,
    masked,
    used_frames,
    tables,
    mask_vec,
    attn_in,
    head_temp,
    attn_out,
    conv_in,
    conv_kernel,
    conv_out,
    voc_in,
    voc_kernel,
    voc_up,
    voc_down,
    voc_head,
    head_bias,
):
    frame_count = tokens.shape[1]
    group_count = lax.axis_size(("head", "sub"))
    group_index = lax.axis_index(("head", "sub"))
    seq_index = lax.axis_index("seq")
    slab_rows = frame_count // group_count
    frame_ceiling = used_frames[0]
    total_frames = frame_count * lax.axis_size("seq")
    masked_rows = masked == 1
    packed = jnp.stack(
        [
            tokens[0],
            tokens[1],
            jnp.where(masked_rows, -1, tokens[2]),
            masked_rows.astype(jnp.int32),
        ],
        axis=1,
    )
    packed = jnp.pad(packed, ((0, 0), (0, 124)))
    embedded, attended, attn_out_full, conv_out_full, voc_in_flat3 = attention(
        used_frames, head_temp, packed, tables, mask_vec, attn_in, (attn_out, conv_out, voc_in), group_count
    )
    fft_size = 2 * (head_bias.shape[0] // 2 - 1)
    intersection = fft_size // HOP
    half_voc = voc_kernel.shape[0] // 2
    vocoder_rim = half_voc + intersection // 2
    conv_reach = conv_kernel.shape[0] // 2 + vocoder_rim
    window_rows = slab_rows + 2 * vocoder_rim
    stream_rows = embedded.astype(jnp.float32) + jnp.einsum(
        "grc,gcd->rd", attended, attn_out_full, preferred_element_type=jnp.float32
    )
    stream_rims = jnp.concatenate(
        [
            stream_rows[frame_count + HALO - conv_reach : frame_count + HALO],
            stream_rows[:frame_count],
            stream_rows[frame_count + HALO : frame_count + HALO + conv_reach],
        ]
    )
    rim_ids = seq_index * frame_count - conv_reach + lax.broadcasted_iota(
        jnp.int32, (frame_count + 2 * conv_reach, 1), 0
    )
    stream_rims = jnp.where((rim_ids >= 0) & (rim_ids < total_frames), stream_rims, 0.0)
    conv_normed = layer_norm(stream_rims).astype(jnp.bfloat16)
    residual_window = lax.dynamic_slice_in_dim(
        stream_rims, group_index * slab_rows + conv_reach - vocoder_rim, window_rows, 0
    )
    gate_value = jnp.dot(conv_normed, conv_in[0], preferred_element_type=jnp.float32)
    gate_signal = jnp.dot(conv_normed, conv_in[1], preferred_element_type=jnp.float32)
    gated_rows = (gate_value * jax.nn.sigmoid(gate_signal)).astype(jnp.bfloat16)
    depth_rows = depthwise(conv_kernel, gated_rows)
    activated = (depth_rows * jax.nn.sigmoid(depth_rows)).astype(jnp.bfloat16)
    windows = jnp.stack(
        [
            activated[member * slab_rows : member * slab_rows + window_rows]
            for member in range(group_count)
        ]
    )
    pad_rows = -window_rows % 16
    windows = jnp.pad(windows, ((0, 0), (0, pad_rows), (0, 0)))
    swapped, voc_up_flat3, voc_down_flat3, voc_head_flat3 = swap(windows, (voc_up, voc_down, voc_head))
    voc_in_flat, voc_up_flat, voc_down_flat, voc_head_flat = (
        full.reshape(-1, full.shape[2])
        for full in (voc_in_flat3, voc_up_flat3, voc_down_flat3, voc_head_flat3)
    )
    conv_sum = jnp.einsum(
        "gsc,gcd->sd", swapped[:, :window_rows], conv_out_full, preferred_element_type=jnp.float32
    )
    block_norm = layer_norm(residual_window + conv_sum).astype(jnp.bfloat16)
    feature_out = block_norm[vocoder_rim : vocoder_rim + slab_rows]
    first_frame = seq_index * frame_count + group_index * slab_rows - vocoder_rim
    frame_ids = first_frame + lax.broadcasted_iota(jnp.int32, (window_rows, 1), 0)
    live_rows = (frame_ids >= 0) & (frame_ids < frame_ceiling)
    base_rows = layer_norm(
        jnp.where(
            live_rows, jnp.dot(block_norm, voc_in_flat, preferred_element_type=jnp.float32), 0.0
        )
    )
    vdepth = depthwise(voc_kernel, base_rows)
    voc_rows = vdepth.shape[0]
    inner_rows = layer_norm(vdepth).astype(jnp.bfloat16)
    hidden = jax.nn.gelu(
        jnp.dot(inner_rows, voc_up_flat, preferred_element_type=jnp.float32), approximate=False
    ).astype(jnp.bfloat16)
    refined = base_rows[half_voc : half_voc + voc_rows] + jnp.dot(
        hidden, voc_down_flat, preferred_element_type=jnp.float32
    )
    head_input = layer_norm(refined).astype(jnp.bfloat16)
    spectrum = jnp.dot(head_input, voc_head_flat, preferred_element_type=jnp.float32) + head_bias
    bin_count = spectrum.shape[1] // 2
    magnitude = jnp.minimum(jnp.exp(spectrum[:, :bin_count]), 100.0)
    phase_rows = spectrum[:, bin_count:]
    coefficients = jnp.concatenate(
        [magnitude * jnp.cos(phase_rows), magnitude * jnp.sin(phase_rows)], axis=1
    )
    sample_ids = lax.broadcasted_iota(jnp.int32, (fft_size,), 0).astype(jnp.float32)
    hann_window = 0.5 - 0.5 * jnp.cos(2.0 * math.pi / fft_size * sample_ids)
    cosine_table, sine_table = synthesis_tables(bin_count, fft_size, hann_window)
    wave_rows = jnp.dot(
        (magnitude * jnp.cos(phase_rows)).astype(jnp.bfloat16), cosine_table, preferred_element_type=jnp.float32
    ) + jnp.dot(
        (magnitude * jnp.sin(phase_rows)).astype(jnp.bfloat16), sine_table, preferred_element_type=jnp.float32
    )
    wave_ids = first_frame + half_voc + lax.broadcasted_iota(jnp.int32, (voc_rows, 1), 0)
    exists = ((wave_ids >= 0) & (wave_ids < total_frames)).astype(jnp.float32)
    framed = (wave_rows * exists).reshape(voc_rows, intersection, HOP)
    env_rows = (exists * (hann_window * hann_window)[None, :]).reshape(voc_rows, intersection, HOP)
    audio_sum = jnp.zeros((slab_rows, HOP), jnp.float32)
    energy = jnp.zeros((slab_rows, HOP), jnp.float32)
    for quarter in range(intersection):
        begin = intersection - quarter
        audio_sum = audio_sum + framed[begin : begin + slab_rows, quarter]
        energy = energy + env_rows[begin : begin + slab_rows, quarter]
    waveform = (audio_sum / energy).reshape(slab_rows * HOP)
    return (feature_out, waveform)


def solution(mesh):
    in_specs = (
        P(None, ("groups", "seq")),
        P(("groups", "seq")),
        P("groups"),
        P(None, None, ("head", "sub")),
        P(("head", "sub")),
        P(None, None, ("head", "sub")),
        P(("head", "sub")),
        P(("head", "sub"), None),
        P(None, None, ("head", "sub")),
        P(None, ("head", "sub")),
        P(("head", "sub"), None),
        P(("head", "sub"), None),
        P(),
        P(("head", "sub"), None),
        P(("head", "sub"), None),
        P(("head", "sub"), None),
        P(),
    )
    out_specs = (P(("groups", "seq", "head", "sub"), None), P(("groups", "seq", "head", "sub")))
    return jax.shard_map(local, mesh=mesh, in_specs=in_specs, out_specs=out_specs, check_vma=False)
```

```python
import functools
import math

import jax
import jax.numpy as jnp
from jax import lax
from jax.experimental import pallas as pl
from jax.experimental.pallas import tpu as pltpu
from jax.sharding import PartitionSpec as P

HOP = 320


def layer_norm(values):
    average = jnp.mean(values, axis=-1, keepdims=True)
    centered = values - average
    return centered * lax.rsqrt(jnp.mean(centered * centered, axis=-1, keepdims=True) + 1e-05)


def depthwise(kernel, padded_rows):
    tap_count = kernel.shape[0]
    out_rows = padded_rows.shape[0] - tap_count + 1
    result = jnp.zeros((out_rows, padded_rows.shape[1]), jnp.float32)
    for offset in range(tap_count):
        result = result + kernel[offset] * padded_rows[offset : offset + out_rows].astype(
            jnp.float32
        )
    return result


def synthesis_tables(bin_count, fft_size, window):
    fine = 16
    coarse = -(-bin_count // fine)
    unit = 2.0 * math.pi / fft_size
    samples = lax.broadcasted_iota(jnp.int32, (coarse, fft_size), 1)
    steps = lax.broadcasted_iota(jnp.int32, (coarse, fft_size), 0) * fine
    big = unit * (steps * samples % fft_size).astype(jnp.float32)
    samples = lax.broadcasted_iota(jnp.int32, (fine, fft_size), 1)
    steps = lax.broadcasted_iota(jnp.int32, (fine, fft_size), 0)
    small = unit * (steps * samples % fft_size).astype(jnp.float32)
    big_cos, big_sin, small_cos, small_sin = lax.optimization_barrier(
        (jnp.cos(big) * window, jnp.sin(big) * window, jnp.cos(small), jnp.sin(small))
    )
    cosine = big_cos[:, None] * small_cos[None] - big_sin[:, None] * small_sin[None]
    sine = big_sin[:, None] * small_cos[None] + big_cos[:, None] * small_sin[None]
    bins = lax.broadcasted_iota(jnp.int32, (coarse * fine, 1), 0)
    edge = (bins == 0) | (bins == bin_count - 1)
    factor = jnp.where(edge, 1.0, 2.0) / fft_size
    cosine = factor * cosine.reshape(coarse * fine, fft_size)
    sine = jnp.where(edge, 0.0, -factor * sine.reshape(coarse * fine, fft_size))
    return cosine[:bin_count].astype(jnp.bfloat16), sine[:bin_count].astype(jnp.bfloat16)


MESH = pl.DeviceIdType.MESH
HALO = 32


def remote(src, dst, send_sem, recv_sem, **where):
    return pltpu.make_async_remote_copy(
        src_ref=src,
        dst_ref=dst,
        send_sem=send_sem,
        recv_sem=recv_sem,
        device_id=where,
        device_id_type=MESH,
    )


class Place:
    def __init__(self):
        self.group, self.seq = lax.axis_index("groups"), lax.axis_index("seq")
        self.head, self.sub = lax.axis_index("head"), lax.axis_index("sub")
        self.groups, self.seqs = lax.axis_size("groups"), lax.axis_size("seq")
        self.heads = lax.axis_size("head")
        self.me = self.head * 2 + self.sub
        self.partner = 1 - self.sub

    def head_at(self, step):
        return lax.rem(self.head + step, self.heads)

    def group_at(self, step):
        return lax.rem(self.group + step, self.groups)


def enter(at, with_seq):
    barrier = pltpu.get_barrier_semaphore()
    for step in range(1, at.heads):
        pl.semaphore_signal(barrier, inc=1, device_id={"head": at.head_at(step)}, device_id_type=MESH)
    for step in range(1, at.groups):
        pl.semaphore_signal(barrier, inc=1, device_id={"groups": at.group_at(step)}, device_id_type=MESH)
    pl.semaphore_signal(barrier, inc=1, device_id={"sub": at.partner}, device_id_type=MESH)
    count = at.heads + at.groups - 1
    if with_seq:

        @pl.when(at.seq > 0)
        def _():
            pl.semaphore_signal(barrier, inc=1, device_id={"seq": at.seq - 1}, device_id_type=MESH)

        @pl.when(at.seq < at.seqs - 1)
        def _():
            pl.semaphore_signal(barrier, inc=1, device_id={"seq": at.seq + 1}, device_id_type=MESH)

        count = (
            count
            + jnp.where(at.seq > 0, 1, 0)
            + jnp.where(at.seq < at.seqs - 1, 1, 0)
        )
    pl.semaphore_wait(barrier, count)


class Spread:
    def __init__(self, at, buffer, rows, sems):
        self.at, self.buffer, self.rows = at, buffer, rows
        self.send, self.recv = sems

    def part(self, block):
        return self.buffer.at[block, pl.ds(*self.rows)]

    def cross(self, step):
        block = self.part(self.at.me)
        return remote(
            block, block, self.send.at[step], self.recv.at[step], head=self.at.head_at(step)
        )

    def aside(self, step):
        block = self.part(self.at.head_at(self.at.heads - step) * 2 + self.at.sub)
        slot = self.at.heads + step
        return remote(block, block, self.send.at[slot], self.recv.at[slot], sub=self.at.partner)

    def start(self):
        for step in range(1, self.at.heads):
            self.cross(step).start()
        self.aside(0).start()

    def relay(self):
        for step in range(1, self.at.heads):
            self.cross(step).wait_recv()
            self.aside(step).start()

    def finish(self):
        for step in range(self.at.heads):
            if step > 0:
                self.cross(step).wait_send()
            self.aside(step).wait()


class Weight:
    def __init__(self, at, own, full, sems):
        self.at, self.own, self.full = at, own, full
        self.send, self.recv, self.local = sems
        self.length = own.shape[0] // at.groups

    def piece(self, block, part):
        start = pl.multiple_of(part * self.length, 16)
        return self.full.at[block, pl.ds(start, self.length)]

    def source(self, step):
        return self.at.head_at(self.at.heads - step) * 2 + self.at.sub

    def cross(self, step):
        start = pl.multiple_of(self.at.group * self.length, 16)
        return remote(
            self.own.at[pl.ds(start, self.length)],
            self.piece(self.at.me, self.at.group),
            self.send.at[step],
            self.recv.at[step],
            head=self.at.head_at(step),
        )

    def over(self, step, turn):
        block = self.piece(self.source(step), self.at.group)
        slot = self.at.heads + (step - 1) * self.at.groups + turn
        return remote(
            block, block, self.send.at[slot], self.recv.at[slot], groups=self.at.group_at(turn)
        )

    def aside(self, step, turn):
        part = self.at.group_at(self.at.groups - turn)
        block = self.piece(self.source(step), part)
        slot = self.at.heads * (1 + self.at.groups) + (step - 1) * self.at.groups + turn
        return remote(block, block, self.send.at[slot], self.recv.at[slot], sub=self.at.partner)

    def mine(self):
        return remote(
            self.own, self.full.at[self.at.me], self.send.at[0], self.recv.at[0], sub=self.at.partner
        )

    def kept(self):
        return pltpu.make_async_copy(self.own, self.full.at[self.at.me], self.local.at[0])

    def start(self):
        for step in range(1, self.at.heads):
            self.cross(step).start()
        self.mine().start()
        self.kept().start()

    def relay_cross(self):
        for step in range(1, self.at.heads):
            self.cross(step).wait_recv()
            for turn in range(1, self.at.groups):
                self.over(step, turn).start()
            self.aside(step, 0).start()

    def relay_over(self):
        for step in range(1, self.at.heads):
            for turn in range(1, self.at.groups):
                self.over(step, turn).wait_recv()
                self.aside(step, turn).start()

    def finish(self):
        self.mine().wait()
        self.kept().wait()
        for step in range(1, self.at.heads):
            self.cross(step).wait_send()
            for turn in range(1, self.at.groups):
                self.over(step, turn).wait_send()
            for turn in range(self.at.groups):
                self.aside(step, turn).wait()


def weight_sems(heads, groups):
    count = heads * (1 + 2 * groups)
    return [
        pltpu.SemaphoreType.DMA((count,)),
        pltpu.SemaphoreType.DMA((count,)),
        pltpu.SemaphoreType.DMA((1,)),
    ]


def norm_rows(values):
    average = jnp.mean(values, axis=-1, keepdims=True)
    centered = values - average
    return centered * lax.rsqrt(jnp.mean(centered * centered, axis=-1, keepdims=True) + 1e-05)


def attention_kernel(weight_count, head_size, *refs):
    used_ref, temp_ref, tok_ref, tables_ref, mask_ref, attn_ref = refs[:6]
    owns = refs[6 : 6 + weight_count]
    refs = refs[6 + weight_count :]
    emb_out, att_out = refs[:2]
    fulls = refs[2 : 2 + weight_count]
    refs = refs[2 + weight_count :]
    (tokh, emb, att, kvbuf, q_scr, acc, l_acc, tok_send, tok_recv, e_send, e_recv, a_send, a_recv,
     r_send, r_recv, l_send, l_recv) = refs[:17]
    wsems = refs[17:]
    at = Place()
    rows = tok_ref.shape[0]
    total = rows + 2 * HALO
    blocks = emb.shape[0]
    codes = tables_ref.shape[1]
    local_heads = q_scr.shape[0]
    width = q_scr.shape[2]
    tokh[...] = jnp.zeros_like(tokh)
    enter(at, True)
    first, last = at.seq == 0, at.seq == at.seqs - 1

    def tokens_up():
        return remote(tok_ref.at[pl.ds(rows - HALO, HALO)], tokh.at[pl.ds(0, HALO)],
                      tok_send.at[0], tok_recv.at[0], seq=at.seq + 1)

    def tokens_down():
        return remote(tok_ref.at[pl.ds(0, HALO)], tokh.at[pl.ds(HALO, HALO)],
                      tok_send.at[1], tok_recv.at[1], seq=at.seq - 1)

    @pl.when(jnp.logical_not(last))
    def _():
        tokens_up().start()

    @pl.when(jnp.logical_not(first))
    def _():
        tokens_down().start()

    weights = [
        Weight(at, owns[w], fulls[w], wsems[3 * w : 3 * w + 3]) for w in range(weight_count)
    ]

    def embed(token_rows):
        count = token_rows.shape[0]
        ids = lax.broadcasted_iota(jnp.int32, (count, codes), 1)
        result = token_rows[:, 3:4].astype(jnp.float32) * mask_ref[...].astype(jnp.float32)
        for level in range(3):
            hot = jnp.where(token_rows[:, level : level + 1] == ids, 1.0, 0.0).astype(jnp.bfloat16)
            result = result + jnp.dot(hot, tables_ref[level], preferred_element_type=jnp.float32)
        return result.astype(jnp.bfloat16)

    half = rows // 2
    cut = half // 2
    spreads = [
        Spread(at, emb, (0, half), (e_send.at[0], e_recv.at[0])),
        Spread(at, emb, (half, total - half), (e_send.at[1], e_recv.at[1])),
    ]
    for chunk in range(2):
        emb[at.me, pl.ds(chunk * cut, cut)] = embed(tok_ref[pl.ds(chunk * cut, cut)])
    spreads[0].start()
    for chunk in range(2, 4):
        emb[at.me, pl.ds(chunk * cut, cut)] = embed(tok_ref[pl.ds(chunk * cut, cut)])

    @pl.when(jnp.logical_not(last))
    def _():
        tokens_up().wait_send()

    @pl.when(jnp.logical_not(first))
    def _():
        tokens_up().wait_recv()
        tokens_down().wait_send()

    @pl.when(jnp.logical_not(last))
    def _():
        tokens_down().wait_recv()

    emb[at.me, pl.ds(rows, 2 * HALO)] = embed(tokh[...])
    spreads[1].start()
    for weight in weights:
        weight.start()

    lanes = lax.broadcasted_iota(jnp.int32, (1, width), 1)
    in_head = [
        (lanes >= h * head_size) & (lanes < (h + 1) * head_size) for h in range(local_heads)
    ]

    def unit(projected):
        squares = projected * projected
        scale = jnp.zeros_like(projected)
        for h in range(local_heads):
            total_h = jnp.sum(jnp.where(in_head[h], squares, 0.0), axis=-1, keepdims=True)
            scale = jnp.where(in_head[h], lax.rsqrt(total_h + 1e-06), scale)
        return projected * scale

    def send_up(block, step, piece):
        view = kvbuf.at[block, piece]
        return remote(view, view, r_send.at[step, piece], r_recv.at[step, piece], seq=at.seq + 1)

    def send_down(block, step, piece):
        view = kvbuf.at[block, piece]
        return remote(view, view, l_send.at[step, piece], l_recv.at[step, piece], seq=at.seq - 1)

    own_kv = kvbuf.at[at.seq]
    for index, spread in enumerate(spreads):
        spread.relay()
        spread.finish()
        begin, count = spread.rows
        piece = count // 2 if count // 2 % 32 == 0 else count
        for offset in range(begin, begin + count, piece):
            size = piece
            whole = jnp.concatenate(
                [emb[block, pl.ds(offset, size)] for block in range(blocks)], axis=1
            )
            emb_out[pl.ds(offset, size)] = whole
            normed = norm_rows(whole.astype(jnp.float32)).astype(jnp.bfloat16)
            query = unit(jnp.dot(normed, attn_ref[0], preferred_element_type=jnp.float32))
            for h in range(local_heads):
                q_scr[h, pl.ds(offset, size)] = jnp.where(in_head[h], query, 0.0).astype(jnp.bfloat16)
            kept = min(size, rows - offset)
            if kept > 0:
                normed = normed[:kept]
                own_kv[index, 0, pl.ds(offset - begin, kept)] = unit(
                    jnp.dot(normed, attn_ref[1], preferred_element_type=jnp.float32)
                ).astype(jnp.bfloat16)
                own_kv[index, 1, pl.ds(offset - begin, kept)] = jnp.dot(
                    normed, attn_ref[2], preferred_element_type=jnp.float32
                ).astype(jnp.bfloat16)

        @pl.when(jnp.logical_not(last))
        def _():
            send_up(at.seq, 0, index).start()

        @pl.when(jnp.logical_not(first))
        def _():
            send_down(at.seq, 0, index).start()

    acc[...] = jnp.zeros_like(acc)
    l_acc[...] = jnp.zeros_like(l_acc)
    tile = total // 3

    def attend(block, piece):
        frame = block * rows + piece * half + lax.broadcasted_iota(jnp.int32, (1, half), 1)
        live = frame < used_ref[0]
        for h in range(local_heads):
            sharp = temp_ref[h] * 1.4426950408889634
            bias = jnp.where(live, -sharp, -1e30)

            def one(index, carry):
                span = pl.ds(pl.multiple_of(index * tile, 64), tile)
                scores = lax.dot_general(
                    q_scr[h, span],
                    kvbuf[block, piece, 0],
                    (((1,), (1,)), ((), ())),
                    preferred_element_type=jnp.float32,
                )
                chance = jnp.exp2(scores * sharp + bias)
                part = chance[:, :128]
                for lane in range(128, half, 128):
                    part = part + chance[:, lane : lane + 128]
                l_acc[h, span] += part
                acc[h, span] += jnp.dot(
                    chance.astype(jnp.bfloat16), kvbuf[block, piece, 1], preferred_element_type=jnp.float32
                )
                return carry

            lax.fori_loop(0, 3, one, 0)

    def exchange(step):
        for piece in range(2):

            @pl.when(step < at.seq)
            def _():
                block = at.seq - 1 - step
                send_up(block, step, piece).wait_recv()

                @pl.when(jnp.logical_not(last))
                def _():
                    send_up(block, step + 1, piece).start()

                attend(block, piece)

            @pl.when(step < at.seqs - 1 - at.seq)
            def _():
                block = at.seq + 1 + step
                send_down(block, step, piece).wait_recv()

                @pl.when(jnp.logical_not(first))
                def _():
                    send_down(block, step + 1, piece).start()

                attend(block, piece)

    def later(step, carry):
        exchange(step)
        return carry

    attend(at.seq, 0)
    attend(at.seq, 1)
    weights[0].relay_cross()
    exchange(0)
    weights[0].relay_over()
    weights[1].relay_cross()
    exchange(1)
    for weight in weights[2:4]:
        weight.relay_cross()
    for weight in weights[1:3]:
        weight.relay_over()
    lax.fori_loop(2, at.seqs - 1, later, 0)
    value = jnp.zeros((total, width), jnp.float32)
    for h in range(local_heads):
        mean = acc[h] / jnp.sum(l_acc[h], axis=-1, keepdims=True)
        value = jnp.where(in_head[h], mean, value)
    att[at.me] = value.astype(jnp.bfloat16)
    gather = Spread(at, att, (0, total), (a_send, a_recv))
    gather.start()
    for weight in weights[4:]:
        weight.relay_cross()
    for weight in weights[3:4]:
        weight.relay_over()
    gather.relay()
    for weight in weights[4:]:
        weight.relay_over()

    def drain(step, carry):
        @pl.when(jnp.logical_not(last) & (step <= at.seq))
        def _():
            for piece in range(2):
                send_up(at.seq - step, step, piece).wait_send()

        @pl.when(jnp.logical_not(first) & (step <= at.seqs - 1 - at.seq))
        def _():
            for piece in range(2):
                send_down(at.seq + step, step, piece).wait_send()

        return carry

    lax.fori_loop(0, at.seqs - 1, drain, 0)
    gather.finish()
    for block in range(blocks):
        att_out[block] = att[block]
    for weight in weights:
        weight.finish()


def attention(used_frames, head_temp, packed, tables, mask_vec, attn_in, owns, blocks):
    groups, heads, seqs = (lax.axis_size(name) for name in ("groups", "head", "seq"))
    rows = packed.shape[0]
    total = rows + 2 * HALO
    width = attn_in.shape[2]
    local_heads = head_temp.shape[0]
    columns = tables.shape[2]
    vmem = pl.BlockSpec(memory_space=pltpu.VMEM)
    smem = pl.BlockSpec(memory_space=pltpu.SMEM)
    dma = pltpu.SemaphoreType.DMA
    sems = []
    for _ in owns:
        sems += weight_sems(heads, groups)
    return pl.pallas_call(
        functools.partial(attention_kernel, len(owns), width // local_heads),
        out_shape=[
            jax.ShapeDtypeStruct((total, columns * blocks), jnp.bfloat16),
            jax.ShapeDtypeStruct((blocks, total, width), jnp.bfloat16),
        ]
        + [jax.ShapeDtypeStruct((blocks,) + own.shape, own.dtype) for own in owns],
        in_specs=[smem, smem] + [vmem] * (4 + len(owns)),
        out_specs=[vmem, vmem] + [pl.BlockSpec(memory_space=pl.ANY)] * len(owns),
        scratch_shapes=[
            pltpu.VMEM((2 * HALO, packed.shape[1]), jnp.int32),
            pltpu.VMEM((blocks, total, columns), jnp.bfloat16),
            pltpu.VMEM((blocks, total, width), jnp.bfloat16),
            pltpu.VMEM((seqs, 2, 2, rows // 2, width), jnp.bfloat16),
            pltpu.VMEM((local_heads, total, width), jnp.bfloat16),
            pltpu.VMEM((local_heads, total, width), jnp.float32),
            pltpu.VMEM((local_heads, total, 128), jnp.float32),
            dma((2,)),
            dma((2,)),
            dma((2, 2 * heads)),
            dma((2, 2 * heads)),
            dma((2 * heads,)),
            dma((2 * heads,)),
            dma((seqs, 2)),
            dma((seqs, 2)),
            dma((seqs, 2)),
            dma((seqs, 2)),
        ]
        + sems,
        compiler_params=pltpu.CompilerParams(collective_id=0, has_side_effects=True, vmem_limit_bytes=60 * 1024 * 1024),
    )(used_frames, head_temp, packed, tables, mask_vec.reshape(1, -1), attn_in, *owns)


def swap_kernel(weight_count, *refs):
    win_ref = refs[0]
    owns = refs[1 : 1 + weight_count]
    out_ref = refs[1 + weight_count]
    fulls = refs[2 + weight_count : 2 + 2 * weight_count]
    act, send, recv = refs[2 + 2 * weight_count : 5 + 2 * weight_count]
    wsems = refs[5 + 2 * weight_count :]
    at = Place()
    blocks = at.heads * 2
    barrier = pltpu.get_barrier_semaphore()
    peers = []
    for step in range(at.heads):
        for other in range(2):
            if step or other:
                peers.append((step, other))
    for step, other in peers:
        pl.semaphore_signal(
            barrier,
            inc=1,
            device_id={"head": at.head_at(step), "sub": lax.rem(at.sub + other, 2)},
            device_id_type=MESH,
        )
    for step in range(1, at.groups):
        pl.semaphore_signal(barrier, inc=1, device_id={"groups": at.group_at(step)}, device_id_type=MESH)
    pl.semaphore_wait(barrier, blocks - 1 + at.groups - 1)
    copies = []
    for slot, (step, other) in enumerate(peers):
        head, sub = at.head_at(step), lax.rem(at.sub + other, 2)
        copies.append(
            remote(win_ref.at[head * 2 + sub], act.at[at.me], send.at[slot], recv.at[slot], head=head, sub=sub)
        )
        copies[-1].start()
    weights = [
        Weight(at, owns[w], fulls[w], wsems[3 * w : 3 * w + 3]) for w in range(weight_count)
    ]
    for weight in weights:
        weight.start()
    act[at.me] = win_ref[at.me]
    for weight in weights:
        weight.relay_cross()
    for weight in weights:
        weight.relay_over()
    for slot, (step, other) in enumerate(peers):
        copies[slot].wait_send()
        source = at.head_at(at.heads - step) * 2 + lax.rem(at.sub + other, 2)
        remote(win_ref.at[source], act.at[source], send.at[slot], recv.at[slot],
               head=at.head_at(step), sub=lax.rem(at.sub + other, 2)).wait_recv()
    out_ref[...] = act[...]
    for weight in weights:
        weight.finish()


def swap(windows, owns):
    groups, heads = lax.axis_size("groups"), lax.axis_size("head")
    vmem = pl.BlockSpec(memory_space=pltpu.VMEM)
    dma = pltpu.SemaphoreType.DMA
    sems = []
    for _ in owns:
        sems += weight_sems(heads, groups)
    blocks = windows.shape[0]
    return pl.pallas_call(
        functools.partial(swap_kernel, len(owns)),
        out_shape=[jax.ShapeDtypeStruct(windows.shape, windows.dtype)]
        + [jax.ShapeDtypeStruct((blocks,) + own.shape, own.dtype) for own in owns],
        in_specs=[vmem] * (1 + len(owns)),
        out_specs=[vmem] + [pl.BlockSpec(memory_space=pl.ANY)] * len(owns),
        scratch_shapes=[
            pltpu.VMEM(windows.shape, windows.dtype),
            dma((blocks,)),
            dma((blocks,)),
        ]
        + sems,
        compiler_params=pltpu.CompilerParams(collective_id=1, has_side_effects=True),
    )(windows, *owns)


def local(
    tokens,
    masked,
    used_frames,
    tables,
    mask_vec,
    attn_in,
    head_temp,
    attn_out,
    conv_in,
    conv_kernel,
    conv_out,
    voc_in,
    voc_kernel,
    voc_up,
    voc_down,
    voc_head,
    head_bias,
):
    frame_count = tokens.shape[1]
    group_count = lax.axis_size(("head", "sub"))
    group_index = lax.axis_index(("head", "sub"))
    seq_index = lax.axis_index("seq")
    slab_rows = frame_count // group_count
    frame_ceiling = used_frames[0]
    total_frames = frame_count * lax.axis_size("seq")
    masked_rows = masked == 1
    packed = jnp.stack(
        [
            tokens[0],
            tokens[1],
            jnp.where(masked_rows, -1, tokens[2]),
            masked_rows.astype(jnp.int32),
        ],
        axis=1,
    )
    packed = jnp.pad(packed, ((0, 0), (0, 124)))
    embedded, attended, *fulls = attention(
        used_frames, head_temp, packed, tables, mask_vec, attn_in, (attn_out, conv_out, voc_in, voc_up, voc_down, voc_head), group_count
    )
    attn_out_full, conv_out_full = fulls[:2]
    fft_size = 2 * (head_bias.shape[0] // 2 - 1)
    intersection = fft_size // HOP
    half_voc = voc_kernel.shape[0] // 2
    vocoder_rim = half_voc + intersection // 2
    conv_reach = conv_kernel.shape[0] // 2 + vocoder_rim
    window_rows = slab_rows + 2 * vocoder_rim
    stream_rows = embedded.astype(jnp.float32) + jnp.einsum(
        "grc,gcd->rd", attended, attn_out_full, preferred_element_type=jnp.float32
    )
    stream_rims = jnp.concatenate(
        [
            stream_rows[frame_count + HALO - conv_reach : frame_count + HALO],
            stream_rows[:frame_count],
            stream_rows[frame_count + HALO : frame_count + HALO + conv_reach],
        ]
    )
    rim_ids = seq_index * frame_count - conv_reach + lax.broadcasted_iota(
        jnp.int32, (frame_count + 2 * conv_reach, 1), 0
    )
    stream_rims = jnp.where((rim_ids >= 0) & (rim_ids < total_frames), stream_rims, 0.0)
    conv_normed = layer_norm(stream_rims).astype(jnp.bfloat16)
    residual_window = lax.dynamic_slice_in_dim(
        stream_rims, group_index * slab_rows + conv_reach - vocoder_rim, window_rows, 0
    )
    gate_value = jnp.dot(conv_normed, conv_in[0], preferred_element_type=jnp.float32)
    gate_signal = jnp.dot(conv_normed, conv_in[1], preferred_element_type=jnp.float32)
    gated_rows = (gate_value * jax.nn.sigmoid(gate_signal)).astype(jnp.bfloat16)
    depth_rows = depthwise(conv_kernel, gated_rows)
    activated = (depth_rows * jax.nn.sigmoid(depth_rows)).astype(jnp.bfloat16)
    windows = jnp.stack(
        [
            activated[member * slab_rows : member * slab_rows + window_rows]
            for member in range(group_count)
        ]
    )
    pad_rows = -window_rows % 16
    windows = jnp.pad(windows, ((0, 0), (0, pad_rows), (0, 0)))
    (swapped,) = swap(windows, ())
    voc_in_flat, voc_up_flat, voc_down_flat, voc_head_flat = (
        full.reshape(-1, full.shape[2])
        for full in fulls[2:]
    )
    conv_sum = jnp.einsum(
        "gsc,gcd->sd", swapped[:, :window_rows], conv_out_full, preferred_element_type=jnp.float32
    )
    block_norm = layer_norm(residual_window + conv_sum).astype(jnp.bfloat16)
    feature_out = block_norm[vocoder_rim : vocoder_rim + slab_rows]
    first_frame = seq_index * frame_count + group_index * slab_rows - vocoder_rim
    frame_ids = first_frame + lax.broadcasted_iota(jnp.int32, (window_rows, 1), 0)
    live_rows = (frame_ids >= 0) & (frame_ids < frame_ceiling)
    base_rows = layer_norm(
        jnp.where(
            live_rows, jnp.dot(block_norm, voc_in_flat, preferred_element_type=jnp.float32), 0.0
        )
    )
    vdepth = depthwise(voc_kernel, base_rows)
    voc_rows = vdepth.shape[0]
    inner_rows = layer_norm(vdepth).astype(jnp.bfloat16)
    hidden = jax.nn.gelu(
        jnp.dot(inner_rows, voc_up_flat, preferred_element_type=jnp.float32), approximate=False
    ).astype(jnp.bfloat16)
    refined = base_rows[half_voc : half_voc + voc_rows] + jnp.dot(
        hidden, voc_down_flat, preferred_element_type=jnp.float32
    )
    head_input = layer_norm(refined).astype(jnp.bfloat16)
    spectrum = jnp.dot(head_input, voc_head_flat, preferred_element_type=jnp.float32) + head_bias
    bin_count = spectrum.shape[1] // 2
    magnitude = jnp.minimum(jnp.exp(spectrum[:, :bin_count]), 100.0)
    phase_rows = spectrum[:, bin_count:]
    coefficients = jnp.concatenate(
        [magnitude * jnp.cos(phase_rows), magnitude * jnp.sin(phase_rows)], axis=1
    )
    sample_ids = lax.broadcasted_iota(jnp.int32, (fft_size,), 0).astype(jnp.float32)
    hann_window = 0.5 - 0.5 * jnp.cos(2.0 * math.pi / fft_size * sample_ids)
    cosine_table, sine_table = synthesis_tables(bin_count, fft_size, hann_window)
    wave_rows = jnp.dot(
        (magnitude * jnp.cos(phase_rows)).astype(jnp.bfloat16), cosine_table, preferred_element_type=jnp.float32
    ) + jnp.dot(
        (magnitude * jnp.sin(phase_rows)).astype(jnp.bfloat16), sine_table, preferred_element_type=jnp.float32
    )
    wave_ids = first_frame + half_voc + lax.broadcasted_iota(jnp.int32, (voc_rows, 1), 0)
    exists = ((wave_ids >= 0) & (wave_ids < total_frames)).astype(jnp.float32)
    framed = (wave_rows * exists).reshape(voc_rows, intersection, HOP)
    env_rows = (exists * (hann_window * hann_window)[None, :]).reshape(voc_rows, intersection, HOP)
    audio_sum = jnp.zeros((slab_rows, HOP), jnp.float32)
    energy = jnp.zeros((slab_rows, HOP), jnp.float32)
    for quarter in range(intersection):
        begin = intersection - quarter
        audio_sum = audio_sum + framed[begin : begin + slab_rows, quarter]
        energy = energy + env_rows[begin : begin + slab_rows, quarter]
    waveform = (audio_sum / energy).reshape(slab_rows * HOP)
    return (feature_out, waveform)


def solution(mesh):
    in_specs = (
        P(None, ("groups", "seq")),
        P(("groups", "seq")),
        P("groups"),
        P(None, None, ("head", "sub")),
        P(("head", "sub")),
        P(None, None, ("head", "sub")),
        P(("head", "sub")),
        P(("head", "sub"), None),
        P(None, None, ("head", "sub")),
        P(None, ("head", "sub")),
        P(("head", "sub"), None),
        P(("head", "sub"), None),
        P(),
        P(("head", "sub"), None),
        P(("head", "sub"), None),
        P(("head", "sub"), None),
        P(),
    )
    out_specs = (P(("groups", "seq", "head", "sub"), None), P(("groups", "seq", "head", "sub")))
    return jax.shard_map(local, mesh=mesh, in_specs=in_specs, out_specs=out_specs, check_vma=False)
```

```python
import functools
import math

import jax
import jax.numpy as jnp
from jax import lax
from jax.experimental import pallas as pl
from jax.experimental.pallas import tpu as pltpu
from jax.sharding import PartitionSpec as P

HOP = 320


def layer_norm(values):
    average = jnp.mean(values, axis=-1, keepdims=True)
    centered = values - average
    return centered * lax.rsqrt(jnp.mean(centered * centered, axis=-1, keepdims=True) + 1e-05)


def depthwise(kernel, padded_rows):
    tap_count = kernel.shape[0]
    out_rows = padded_rows.shape[0] - tap_count + 1
    result = jnp.zeros((out_rows, padded_rows.shape[1]), jnp.float32)
    for offset in range(tap_count):
        result = result + kernel[offset] * padded_rows[offset : offset + out_rows].astype(
            jnp.float32
        )
    return result


def synthesis_tables(bin_count, fft_size, parts, window):
    fine = 16
    coarse = -(-bin_count // fine)
    hop = fft_size // parts
    unit = 2.0 * math.pi / fft_size

    def angles(count, stride):
        shape = (parts, count, hop)
        samples = lax.broadcasted_iota(jnp.int32, shape, 0) * hop + lax.broadcasted_iota(
            jnp.int32, shape, 2
        )
        steps = lax.broadcasted_iota(jnp.int32, shape, 1) * stride
        return unit * (steps * samples % fft_size).astype(jnp.float32)

    big, small = angles(coarse, fine), angles(fine, 1)
    window = window.reshape(parts, 1, hop)
    big_cos, big_sin, small_cos, small_sin = lax.optimization_barrier(
        (jnp.cos(big) * window, jnp.sin(big) * window, jnp.cos(small), jnp.sin(small))
    )
    cosine = big_cos[:, :, None] * small_cos[:, None] - big_sin[:, :, None] * small_sin[:, None]
    sine = big_sin[:, :, None] * small_cos[:, None] + big_cos[:, :, None] * small_sin[:, None]
    bins = lax.broadcasted_iota(jnp.int32, (1, coarse * fine, 1), 1)
    edge = (bins == 0) | (bins == bin_count - 1)
    factor = jnp.where(edge, 1.0, 2.0) / fft_size
    cosine = factor * cosine.reshape(parts, coarse * fine, hop)
    sine = jnp.where(edge, 0.0, -factor * sine.reshape(parts, coarse * fine, hop))
    return cosine[:, :bin_count].astype(jnp.bfloat16), sine[:, :bin_count].astype(jnp.bfloat16)


MESH = pl.DeviceIdType.MESH
HALO = 32


def remote(src, dst, send_sem, recv_sem, **where):
    return pltpu.make_async_remote_copy(
        src_ref=src,
        dst_ref=dst,
        send_sem=send_sem,
        recv_sem=recv_sem,
        device_id=where,
        device_id_type=MESH,
    )


class Place:
    def __init__(self):
        self.group, self.seq = lax.axis_index("groups"), lax.axis_index("seq")
        self.head, self.sub = lax.axis_index("head"), lax.axis_index("sub")
        self.groups, self.seqs = lax.axis_size("groups"), lax.axis_size("seq")
        self.heads = lax.axis_size("head")
        self.me = self.head * 2 + self.sub
        self.partner = 1 - self.sub

    def head_at(self, step):
        return lax.rem(self.head + step, self.heads)

    def group_at(self, step):
        return lax.rem(self.group + step, self.groups)


def enter(at, with_seq):
    barrier = pltpu.get_barrier_semaphore()
    for step in range(1, at.heads):
        pl.semaphore_signal(barrier, inc=1, device_id={"head": at.head_at(step)}, device_id_type=MESH)
    for step in range(1, at.groups):
        pl.semaphore_signal(barrier, inc=1, device_id={"groups": at.group_at(step)}, device_id_type=MESH)
    pl.semaphore_signal(barrier, inc=1, device_id={"sub": at.partner}, device_id_type=MESH)
    count = at.heads + at.groups - 1
    if with_seq:

        @pl.when(at.seq > 0)
        def _():
            pl.semaphore_signal(barrier, inc=1, device_id={"seq": at.seq - 1}, device_id_type=MESH)

        @pl.when(at.seq < at.seqs - 1)
        def _():
            pl.semaphore_signal(barrier, inc=1, device_id={"seq": at.seq + 1}, device_id_type=MESH)

        count = (
            count
            + jnp.where(at.seq > 0, 1, 0)
            + jnp.where(at.seq < at.seqs - 1, 1, 0)
        )
    pl.semaphore_wait(barrier, count)


class Spread:
    def __init__(self, at, buffer, rows, sems):
        self.at, self.buffer, self.rows = at, buffer, rows
        self.send, self.recv = sems

    def part(self, block):
        return self.buffer.at[block, pl.ds(*self.rows)]

    def cross(self, step):
        block = self.part(self.at.me)
        return remote(
            block, block, self.send.at[step], self.recv.at[step], head=self.at.head_at(step)
        )

    def aside(self, step):
        block = self.part(self.at.head_at(self.at.heads - step) * 2 + self.at.sub)
        slot = self.at.heads + step
        return remote(block, block, self.send.at[slot], self.recv.at[slot], sub=self.at.partner)

    def start(self):
        for step in range(1, self.at.heads):
            self.cross(step).start()
        self.aside(0).start()

    def relay(self):
        for step in range(1, self.at.heads):
            self.cross(step).wait_recv()
            self.aside(step).start()

    def finish(self):
        for step in range(self.at.heads):
            if step > 0:
                self.cross(step).wait_send()
            self.aside(step).wait()


class Weight:
    def __init__(self, at, own, full, sems):
        self.at, self.own, self.full = at, own, full
        self.send, self.recv, self.local = sems
        self.length = own.shape[0] // at.groups

    def piece(self, block, part):
        start = pl.multiple_of(part * self.length, 16)
        return self.full.at[block, pl.ds(start, self.length)]

    def source(self, step):
        return self.at.head_at(self.at.heads - step) * 2 + self.at.sub

    def cross(self, step):
        start = pl.multiple_of(self.at.group * self.length, 16)
        return remote(
            self.own.at[pl.ds(start, self.length)],
            self.piece(self.at.me, self.at.group),
            self.send.at[step],
            self.recv.at[step],
            head=self.at.head_at(step),
        )

    def over(self, step, turn):
        block = self.piece(self.source(step), self.at.group)
        slot = self.at.heads + (step - 1) * self.at.groups + turn
        return remote(
            block, block, self.send.at[slot], self.recv.at[slot], groups=self.at.group_at(turn)
        )

    def aside(self, step, turn):
        part = self.at.group_at(self.at.groups - turn)
        block = self.piece(self.source(step), part)
        slot = self.at.heads * (1 + self.at.groups) + (step - 1) * self.at.groups + turn
        return remote(block, block, self.send.at[slot], self.recv.at[slot], sub=self.at.partner)

    def mine(self):
        return remote(
            self.own, self.full.at[self.at.me], self.send.at[0], self.recv.at[0], sub=self.at.partner
        )

    def kept(self):
        return pltpu.make_async_copy(self.own, self.full.at[self.at.me], self.local.at[0])

    def start(self):
        for step in range(1, self.at.heads):
            self.cross(step).start()
        self.mine().start()
        self.kept().start()

    def relay_cross(self):
        for step in range(1, self.at.heads):
            self.cross(step).wait_recv()
            for turn in range(1, self.at.groups):
                self.over(step, turn).start()
            self.aside(step, 0).start()

    def relay_over(self):
        for step in range(1, self.at.heads):
            for turn in range(1, self.at.groups):
                self.over(step, turn).wait_recv()
                self.aside(step, turn).start()

    def finish(self):
        self.mine().wait()
        self.kept().wait()
        for step in range(1, self.at.heads):
            self.cross(step).wait_send()
            for turn in range(1, self.at.groups):
                self.over(step, turn).wait_send()
            for turn in range(self.at.groups):
                self.aside(step, turn).wait()


def weight_sems(heads, groups):
    count = heads * (1 + 2 * groups)
    return [
        pltpu.SemaphoreType.DMA((count,)),
        pltpu.SemaphoreType.DMA((count,)),
        pltpu.SemaphoreType.DMA((1,)),
    ]


def norm_rows(values):
    average = jnp.mean(values, axis=-1, keepdims=True)
    centered = values - average
    return centered * lax.rsqrt(jnp.mean(centered * centered, axis=-1, keepdims=True) + 1e-05)


def attention_kernel(weight_count, head_size, *refs):
    used_ref, temp_ref, tok_ref, tables_ref, mask_ref, attn_ref = refs[:6]
    owns = refs[6 : 6 + weight_count]
    refs = refs[6 + weight_count :]
    emb_out, att_out = refs[:2]
    fulls = refs[2 : 2 + weight_count]
    refs = refs[2 + weight_count :]
    (tokh, emb, att, kvbuf, q_scr, acc, l_acc, tok_send, tok_recv, e_send, e_recv, a_send, a_recv,
     r_send, r_recv, l_send, l_recv) = refs[:17]
    wsems = refs[17:]
    at = Place()
    rows = tok_ref.shape[0]
    total = rows + 2 * HALO
    blocks = emb.shape[0]
    codes = tables_ref.shape[1]
    local_heads = q_scr.shape[0]
    width = q_scr.shape[2]
    tokh[...] = jnp.zeros_like(tokh)
    enter(at, True)
    first, last = at.seq == 0, at.seq == at.seqs - 1

    def tokens_up():
        return remote(tok_ref.at[pl.ds(rows - HALO, HALO)], tokh.at[pl.ds(0, HALO)],
                      tok_send.at[0], tok_recv.at[0], seq=at.seq + 1)

    def tokens_down():
        return remote(tok_ref.at[pl.ds(0, HALO)], tokh.at[pl.ds(HALO, HALO)],
                      tok_send.at[1], tok_recv.at[1], seq=at.seq - 1)

    @pl.when(jnp.logical_not(last))
    def _():
        tokens_up().start()

    @pl.when(jnp.logical_not(first))
    def _():
        tokens_down().start()

    weights = [
        Weight(at, owns[w], fulls[w], wsems[3 * w : 3 * w + 3]) for w in range(weight_count)
    ]

    def embed(token_rows):
        count = token_rows.shape[0]
        ids = lax.broadcasted_iota(jnp.int32, (count, codes), 1)
        result = token_rows[:, 3:4].astype(jnp.float32) * mask_ref[...].astype(jnp.float32)
        for level in range(3):
            hot = jnp.where(token_rows[:, level : level + 1] == ids, 1.0, 0.0).astype(jnp.bfloat16)
            result = result + jnp.dot(hot, tables_ref[level], preferred_element_type=jnp.float32)
        return result.astype(jnp.bfloat16)

    half = rows // 2
    cut = half // 2
    spreads = [
        Spread(at, emb, (0, half), (e_send.at[0], e_recv.at[0])),
        Spread(at, emb, (half, total - half), (e_send.at[1], e_recv.at[1])),
    ]
    for chunk in range(2):
        emb[at.me, pl.ds(chunk * cut, cut)] = embed(tok_ref[pl.ds(chunk * cut, cut)])
    spreads[0].start()
    for chunk in range(2, 4):
        emb[at.me, pl.ds(chunk * cut, cut)] = embed(tok_ref[pl.ds(chunk * cut, cut)])

    @pl.when(jnp.logical_not(last))
    def _():
        tokens_up().wait_send()

    @pl.when(jnp.logical_not(first))
    def _():
        tokens_up().wait_recv()
        tokens_down().wait_send()

    @pl.when(jnp.logical_not(last))
    def _():
        tokens_down().wait_recv()

    emb[at.me, pl.ds(rows, 2 * HALO)] = embed(tokh[...])
    spreads[1].start()
    for weight in weights:
        weight.start()

    lanes = lax.broadcasted_iota(jnp.int32, (1, width), 1)
    in_head = [
        (lanes >= h * head_size) & (lanes < (h + 1) * head_size) for h in range(local_heads)
    ]

    def unit(projected):
        squares = projected * projected
        scale = jnp.zeros_like(projected)
        for h in range(local_heads):
            total_h = jnp.sum(jnp.where(in_head[h], squares, 0.0), axis=-1, keepdims=True)
            scale = jnp.where(in_head[h], lax.rsqrt(total_h + 1e-06), scale)
        return projected * scale

    def send_up(block, step, piece):
        view = kvbuf.at[block, piece]
        return remote(view, view, r_send.at[step, piece], r_recv.at[step, piece], seq=at.seq + 1)

    def send_down(block, step, piece):
        view = kvbuf.at[block, piece]
        return remote(view, view, l_send.at[step, piece], l_recv.at[step, piece], seq=at.seq - 1)

    segments = (
        (0, rows, HALO),
        (rows, rows + HALO, -rows),
        (rows + HALO, total, 0),
    )
    own_kv = kvbuf.at[at.seq]
    for index, spread in enumerate(spreads):
        spread.relay()
        spread.finish()
        begin, count = spread.rows
        piece = count // 2 if count // 2 % 32 == 0 else count
        for offset in range(begin, begin + count, piece):
            size = piece
            whole = jnp.concatenate(
                [emb[block, pl.ds(offset, size)] for block in range(blocks)], axis=1
            )
            for begin_at, stop_at, shift in segments:
                low, high = max(offset, begin_at), min(offset + size, stop_at)
                if low < high:
                    emb_out[pl.ds(low + shift, high - low)] = whole[low - offset : high - offset]
            normed = norm_rows(whole.astype(jnp.float32)).astype(jnp.bfloat16)
            query = unit(jnp.dot(normed, attn_ref[0], preferred_element_type=jnp.float32))
            for h in range(local_heads):
                q_scr[h, pl.ds(offset, size)] = jnp.where(in_head[h], query, 0.0).astype(jnp.bfloat16)
            kept = min(size, rows - offset)
            if kept > 0:
                normed = normed[:kept]
                own_kv[index, 0, pl.ds(offset - begin, kept)] = unit(
                    jnp.dot(normed, attn_ref[1], preferred_element_type=jnp.float32)
                ).astype(jnp.bfloat16)
                own_kv[index, 1, pl.ds(offset - begin, kept)] = jnp.dot(
                    normed, attn_ref[2], preferred_element_type=jnp.float32
                ).astype(jnp.bfloat16)

        @pl.when(jnp.logical_not(last))
        def _():
            send_up(at.seq, 0, index).start()

        @pl.when(jnp.logical_not(first))
        def _():
            send_down(at.seq, 0, index).start()

    acc[...] = jnp.zeros_like(acc)
    l_acc[...] = jnp.zeros_like(l_acc)
    tile = total // 3

    def attend(block, piece):
        frame = block * rows + piece * half + lax.broadcasted_iota(jnp.int32, (1, half), 1)
        live = frame < used_ref[0]
        for h in range(local_heads):
            sharp = temp_ref[h] * 1.4426950408889634
            bias = jnp.where(live, -sharp, -1e30)

            def one(index, carry):
                span = pl.ds(pl.multiple_of(index * tile, 64), tile)
                scores = lax.dot_general(
                    q_scr[h, span],
                    kvbuf[block, piece, 0],
                    (((1,), (1,)), ((), ())),
                    preferred_element_type=jnp.float32,
                )
                chance = jnp.exp2(scores * sharp + bias)
                part = chance[:, :128]
                for lane in range(128, half, 128):
                    part = part + chance[:, lane : lane + 128]
                l_acc[h, span] += part
                acc[h, span] += jnp.dot(
                    chance.astype(jnp.bfloat16), kvbuf[block, piece, 1], preferred_element_type=jnp.float32
                )
                return carry

            lax.fori_loop(0, 3, one, 0)

    def exchange(step):
        for piece in range(2):

            @pl.when(step < at.seq)
            def _():
                block = at.seq - 1 - step
                send_up(block, step, piece).wait_recv()

                @pl.when(jnp.logical_not(last))
                def _():
                    send_up(block, step + 1, piece).start()

                attend(block, piece)

            @pl.when(step < at.seqs - 1 - at.seq)
            def _():
                block = at.seq + 1 + step
                send_down(block, step, piece).wait_recv()

                @pl.when(jnp.logical_not(first))
                def _():
                    send_down(block, step + 1, piece).start()

                attend(block, piece)

    def later(step, carry):
        exchange(step)
        return carry

    attend(at.seq, 0)
    attend(at.seq, 1)
    weights[0].relay_cross()
    exchange(0)
    weights[0].relay_over()
    weights[1].relay_cross()
    exchange(1)
    for weight in weights[2:4]:
        weight.relay_cross()
    for weight in weights[1:3]:
        weight.relay_over()
    lax.fori_loop(2, at.seqs - 1, later, 0)
    value = jnp.zeros((total, width), jnp.float32)
    for h in range(local_heads):
        mean = acc[h] / jnp.sum(l_acc[h], axis=-1, keepdims=True)
        value = jnp.where(in_head[h], mean, value)
    att[at.me] = value.astype(jnp.bfloat16)
    gather = Spread(at, att, (0, total), (a_send, a_recv))
    gather.start()
    for weight in weights[4:]:
        weight.relay_cross()
    for weight in weights[3:4]:
        weight.relay_over()
    gather.relay()
    for weight in weights[4:]:
        weight.relay_over()

    def drain(step, carry):
        @pl.when(jnp.logical_not(last) & (step <= at.seq))
        def _():
            for piece in range(2):
                send_up(at.seq - step, step, piece).wait_send()

        @pl.when(jnp.logical_not(first) & (step <= at.seqs - 1 - at.seq))
        def _():
            for piece in range(2):
                send_down(at.seq + step, step, piece).wait_send()

        return carry

    lax.fori_loop(0, at.seqs - 1, drain, 0)
    gather.finish()
    for block in range(blocks):
        for begin_at, stop_at, shift in segments:
            span = pl.ds(begin_at + shift, stop_at - begin_at)
            att_out[block, span] = att[block, pl.ds(begin_at, stop_at - begin_at)]
    for weight in weights:
        weight.finish()


def attention(used_frames, head_temp, packed, tables, mask_vec, attn_in, owns, blocks):
    groups, heads, seqs = (lax.axis_size(name) for name in ("groups", "head", "seq"))
    rows = packed.shape[0]
    total = rows + 2 * HALO
    width = attn_in.shape[2]
    local_heads = head_temp.shape[0]
    columns = tables.shape[2]
    vmem = pl.BlockSpec(memory_space=pltpu.VMEM)
    smem = pl.BlockSpec(memory_space=pltpu.SMEM)
    dma = pltpu.SemaphoreType.DMA
    sems = []
    for _ in owns:
        sems += weight_sems(heads, groups)
    return pl.pallas_call(
        functools.partial(attention_kernel, len(owns), width // local_heads),
        out_shape=[
            jax.ShapeDtypeStruct((total, columns * blocks), jnp.bfloat16),
            jax.ShapeDtypeStruct((blocks, total, width), jnp.bfloat16),
        ]
        + [jax.ShapeDtypeStruct((blocks,) + own.shape, own.dtype) for own in owns],
        in_specs=[smem, smem] + [vmem] * (4 + len(owns)),
        out_specs=[vmem, vmem] + [pl.BlockSpec(memory_space=pl.ANY)] * len(owns),
        scratch_shapes=[
            pltpu.VMEM((2 * HALO, packed.shape[1]), jnp.int32),
            pltpu.VMEM((blocks, total, columns), jnp.bfloat16),
            pltpu.VMEM((blocks, total, width), jnp.bfloat16),
            pltpu.VMEM((seqs, 2, 2, rows // 2, width), jnp.bfloat16),
            pltpu.VMEM((local_heads, total, width), jnp.bfloat16),
            pltpu.VMEM((local_heads, total, width), jnp.float32),
            pltpu.VMEM((local_heads, total, 128), jnp.float32),
            dma((2,)),
            dma((2,)),
            dma((2, 2 * heads)),
            dma((2, 2 * heads)),
            dma((2 * heads,)),
            dma((2 * heads,)),
            dma((seqs, 2)),
            dma((seqs, 2)),
            dma((seqs, 2)),
            dma((seqs, 2)),
        ]
        + sems,
        compiler_params=pltpu.CompilerParams(collective_id=0, has_side_effects=True, vmem_limit_bytes=60 * 1024 * 1024),
    )(used_frames, head_temp, packed, tables, mask_vec.reshape(1, -1), attn_in, *owns)


def swap_kernel(weight_count, *refs):
    win_ref = refs[0]
    owns = refs[1 : 1 + weight_count]
    out_ref = refs[1 + weight_count]
    fulls = refs[2 + weight_count : 2 + 2 * weight_count]
    act, send, recv = refs[2 + 2 * weight_count : 5 + 2 * weight_count]
    wsems = refs[5 + 2 * weight_count :]
    at = Place()
    blocks = at.heads * 2
    barrier = pltpu.get_barrier_semaphore()
    peers = []
    for step in range(at.heads):
        for other in range(2):
            if step or other:
                peers.append((step, other))
    for step, other in peers:
        pl.semaphore_signal(
            barrier,
            inc=1,
            device_id={"head": at.head_at(step), "sub": lax.rem(at.sub + other, 2)},
            device_id_type=MESH,
        )
    for step in range(1, at.groups):
        pl.semaphore_signal(barrier, inc=1, device_id={"groups": at.group_at(step)}, device_id_type=MESH)
    pl.semaphore_wait(barrier, blocks - 1 + at.groups - 1)
    copies = []
    for slot, (step, other) in enumerate(peers):
        head, sub = at.head_at(step), lax.rem(at.sub + other, 2)
        copies.append(
            remote(win_ref.at[head * 2 + sub], act.at[at.me], send.at[slot], recv.at[slot], head=head, sub=sub)
        )
        copies[-1].start()
    weights = [
        Weight(at, owns[w], fulls[w], wsems[3 * w : 3 * w + 3]) for w in range(weight_count)
    ]
    for weight in weights:
        weight.start()
    act[at.me] = win_ref[at.me]
    for weight in weights:
        weight.relay_cross()
    for weight in weights:
        weight.relay_over()
    for slot, (step, other) in enumerate(peers):
        copies[slot].wait_send()
        source = at.head_at(at.heads - step) * 2 + lax.rem(at.sub + other, 2)
        remote(win_ref.at[source], act.at[source], send.at[slot], recv.at[slot],
               head=at.head_at(step), sub=lax.rem(at.sub + other, 2)).wait_recv()
    out_ref[...] = act[...]
    for weight in weights:
        weight.finish()


def swap(windows, owns):
    groups, heads = lax.axis_size("groups"), lax.axis_size("head")
    vmem = pl.BlockSpec(memory_space=pltpu.VMEM)
    dma = pltpu.SemaphoreType.DMA
    sems = []
    for _ in owns:
        sems += weight_sems(heads, groups)
    blocks = windows.shape[0]
    return pl.pallas_call(
        functools.partial(swap_kernel, len(owns)),
        out_shape=[jax.ShapeDtypeStruct(windows.shape, windows.dtype)]
        + [jax.ShapeDtypeStruct((blocks,) + own.shape, own.dtype) for own in owns],
        in_specs=[vmem] * (1 + len(owns)),
        out_specs=[vmem] + [pl.BlockSpec(memory_space=pl.ANY)] * len(owns),
        scratch_shapes=[
            pltpu.VMEM(windows.shape, windows.dtype),
            dma((blocks,)),
            dma((blocks,)),
        ]
        + sems,
        compiler_params=pltpu.CompilerParams(collective_id=1, has_side_effects=True),
    )(windows, *owns)


def local(
    tokens,
    masked,
    used_frames,
    tables,
    mask_vec,
    attn_in,
    head_temp,
    attn_out,
    conv_in,
    conv_kernel,
    conv_out,
    voc_in,
    voc_kernel,
    voc_up,
    voc_down,
    voc_head,
    head_bias,
):
    frame_count = tokens.shape[1]
    group_count = lax.axis_size(("head", "sub"))
    group_index = lax.axis_index(("head", "sub"))
    seq_index = lax.axis_index("seq")
    slab_rows = frame_count // group_count
    frame_ceiling = used_frames[0]
    total_frames = frame_count * lax.axis_size("seq")
    masked_rows = masked == 1
    packed = jnp.stack(
        [
            tokens[0],
            tokens[1],
            jnp.where(masked_rows, -1, tokens[2]),
            masked_rows.astype(jnp.int32),
        ],
        axis=1,
    )
    packed = jnp.pad(packed, ((0, 0), (0, 124)))
    embedded, attended, *fulls = attention(
        used_frames, head_temp, packed, tables, mask_vec, attn_in, (attn_out, conv_out, voc_in, voc_up, voc_down, voc_head), group_count
    )
    attn_out_full, conv_out_full = fulls[:2]
    fft_size = 2 * (head_bias.shape[0] // 2 - 1)
    intersection = fft_size // HOP
    half_voc = voc_kernel.shape[0] // 2
    vocoder_rim = half_voc + intersection // 2
    conv_reach = conv_kernel.shape[0] // 2 + vocoder_rim
    window_rows = slab_rows + 2 * vocoder_rim
    stream_rows = embedded.astype(jnp.float32) + jnp.einsum(
        "grc,gcd->rd", attended, attn_out_full, preferred_element_type=jnp.float32
    )
    rim_ids = seq_index * frame_count - HALO + lax.broadcasted_iota(
        jnp.int32, (frame_count + 2 * HALO, 1), 0
    )
    stream_rims = jnp.where((rim_ids >= 0) & (rim_ids < total_frames), stream_rows, 0.0)
    conv_normed = layer_norm(stream_rims).astype(jnp.bfloat16)
    residual_window = lax.dynamic_slice_in_dim(
        stream_rims, group_index * slab_rows + HALO - vocoder_rim, window_rows, 0
    )
    gate_value = jnp.dot(conv_normed, conv_in[0], preferred_element_type=jnp.float32)
    gate_signal = jnp.dot(conv_normed, conv_in[1], preferred_element_type=jnp.float32)
    gated_rows = (gate_value * jax.nn.sigmoid(gate_signal)).astype(jnp.bfloat16)
    depth_rows = depthwise(conv_kernel, gated_rows)
    activated = (depth_rows * jax.nn.sigmoid(depth_rows)).astype(jnp.bfloat16)
    first = HALO - conv_reach
    windows = jnp.stack(
        [
            activated[first + member * slab_rows : first + member * slab_rows + window_rows]
            for member in range(group_count)
        ]
    )
    pad_rows = -window_rows % 16
    windows = jnp.pad(windows, ((0, 0), (0, pad_rows), (0, 0)))
    (swapped,) = swap(windows, ())
    voc_in_flat, voc_up_flat, voc_down_flat, voc_head_flat = (
        full.reshape(-1, full.shape[2])
        for full in fulls[2:]
    )
    conv_sum = jnp.einsum(
        "gsc,gcd->sd", swapped[:, :window_rows], conv_out_full, preferred_element_type=jnp.float32
    )
    block_norm = layer_norm(residual_window + conv_sum).astype(jnp.bfloat16)
    feature_out = block_norm[vocoder_rim : vocoder_rim + slab_rows]
    first_frame = seq_index * frame_count + group_index * slab_rows - vocoder_rim
    frame_ids = first_frame + lax.broadcasted_iota(jnp.int32, (window_rows, 1), 0)
    live_rows = (frame_ids >= 0) & (frame_ids < frame_ceiling)
    base_rows = layer_norm(
        jnp.where(
            live_rows, jnp.dot(block_norm, voc_in_flat, preferred_element_type=jnp.float32), 0.0
        )
    )
    vdepth = depthwise(voc_kernel, base_rows)
    voc_rows = vdepth.shape[0]
    inner_rows = layer_norm(vdepth).astype(jnp.bfloat16)
    hidden = jax.nn.gelu(
        jnp.dot(inner_rows, voc_up_flat, preferred_element_type=jnp.float32), approximate=False
    ).astype(jnp.bfloat16)
    refined = base_rows[half_voc : half_voc + voc_rows] + jnp.dot(
        hidden, voc_down_flat, preferred_element_type=jnp.float32
    )
    head_input = layer_norm(refined).astype(jnp.bfloat16)
    spectrum = jnp.dot(head_input, voc_head_flat, preferred_element_type=jnp.float32) + head_bias
    bin_count = spectrum.shape[1] // 2
    magnitude = jnp.minimum(jnp.exp(spectrum[:, :bin_count]), 100.0)
    phase_rows = spectrum[:, bin_count:]
    sample_ids = lax.broadcasted_iota(jnp.int32, (fft_size,), 0).astype(jnp.float32)
    hann_window = 0.5 - 0.5 * jnp.cos(2.0 * math.pi / fft_size * sample_ids)
    cosine_table, sine_table = synthesis_tables(bin_count, fft_size, intersection, hann_window)
    wave_ids = first_frame + half_voc + lax.broadcasted_iota(jnp.int32, (voc_rows, 1), 0)
    exists = (wave_ids >= 0) & (wave_ids < total_frames)
    magnitude = jnp.where(exists, magnitude, 0.0)
    real_rows = (magnitude * jnp.cos(phase_rows)).astype(jnp.bfloat16)
    imag_rows = (magnitude * jnp.sin(phase_rows)).astype(jnp.bfloat16)
    env_rows = (exists.astype(jnp.float32) * (hann_window * hann_window)[None, :]).reshape(
        voc_rows, intersection, HOP
    )
    audio_sum = jnp.zeros((slab_rows, HOP), jnp.float32)
    energy = jnp.zeros((slab_rows, HOP), jnp.float32)
    for quarter in range(intersection):
        begin = intersection - quarter
        for part_rows, table in ((real_rows, cosine_table), (imag_rows, sine_table)):
            audio_sum = audio_sum + jnp.dot(
                part_rows[begin : begin + slab_rows],
                table[quarter],
                preferred_element_type=jnp.float32,
            )
        energy = energy + env_rows[begin : begin + slab_rows, quarter]
    waveform = (audio_sum / energy).reshape(slab_rows * HOP)
    return (feature_out, waveform)


def solution(mesh):
    in_specs = (
        P(None, ("groups", "seq")),
        P(("groups", "seq")),
        P("groups"),
        P(None, None, ("head", "sub")),
        P(("head", "sub")),
        P(None, None, ("head", "sub")),
        P(("head", "sub")),
        P(("head", "sub"), None),
        P(None, None, ("head", "sub")),
        P(None, ("head", "sub")),
        P(("head", "sub"), None),
        P(("head", "sub"), None),
        P(),
        P(("head", "sub"), None),
        P(("head", "sub"), None),
        P(("head", "sub"), None),
        P(),
    )
    out_specs = (P(("groups", "seq", "head", "sub"), None), P(("groups", "seq", "head", "sub")))
    return jax.shard_map(local, mesh=mesh, in_specs=in_specs, out_specs=out_specs, check_vma=False)
```
